128 devices in a mesh: dp: 64 (over x, z_hi, y, core), tensor: 2 (over z_lo).
Axes of the slice: x: 4, y: 4, z: 4 (z_hi: 2, z_lo: 2; z = z_hi * 2 + z_lo), core: 2. Of those that a mesh axis runs over, the one named last changes fastest.
Arguments:
- inputs: bfloat16 [16384, 1152], P(('dp', 'tensor')), may hold values from -24 to 24
- doc_ids: int32 [64, 256], P('dp'), may hold values from 0 to 3, never falling along the last dimension, each value on 1 to 128 neighbouring positions
- prenorm: bfloat16 [1152], P('dp'), may hold values from 0.099609375 to 1.8984375
- query_proj: bfloat16 [1152, 1024], P('dp', 'tensor'), may hold values from -0.1875 to 0.1875
- key_proj: bfloat16 [1152, 256], P('dp'), may hold values from -0.1875 to 0.1875
- value_proj: bfloat16 [1152, 256], P('dp'), may hold values from -0.1875 to 0.1875
- querynorm: bfloat16 [256], P('dp'), may hold values from 0.5 to 2
- keynorm: bfloat16 [256], P('dp'), may hold values from 0.5 to 2
- output_proj: bfloat16 [1024, 1152], P('tensor', 'dp'), may hold values from -0.1875 to 0.1875
- postnorm: bfloat16 [1152], P('dp'), may hold values from 0.099609375 to 1.8984375
- ffnnorm: bfloat16 [1152], P('dp'), may hold values from 0.099609375 to 1.8984375
- gate_proj: bfloat16 [1152, 6912], P('dp', 'tensor'), may hold values from -0.1875 to 0.1875
- up_proj: bfloat16 [1152, 6912], P('dp', 'tensor'), may hold values from -0.1875 to 0.1875
- down_proj: bfloat16 [6912, 1152], P('tensor', 'dp'), may hold values from -0.078125 to 0.078125
- endnorm: bfloat16 [1152], P('dp'), may hold values from 0.099609375 to 1.8984375
- cotangent: bfloat16 [16384, 1152], P(('dp', 'tensor')), may hold values from -24 to 24
Outputs:
- layer_out: bfloat16 [16384, 1152], P(('dp', 'tensor'))
- inputs_grad: float32 [16384, 1152], P(('dp', 'tensor'))
- prenorm_grad: float32 [1152], P('dp')
- query_grad: float32 [1152, 1024], P('dp', 'tensor')
- key_grad: float32 [1152, 256], P('dp')
- value_grad: float32 [1152, 256], P('dp')
- querynorm_grad: float32 [256], P('dp')
- keynorm_grad: float32 [256], P('dp')
- output_grad: float32 [1024, 1152], P('tensor', 'dp')
- postnorm_grad: float32 [1152], P('dp')
- ffnnorm_grad: float32 [1152], P('dp')
- gate_grad: float32 [1152, 6912], P('dp', 'tensor')
- up_grad: float32 [1152, 6912], P('dp', 'tensor')
- down_grad: float32 [6912, 1152], P('tensor', 'dp')
- endnorm_grad: float32 [1152], P('dp')
The draws below stay inside these ranges and needn't reach their ends.
Inputs may be any that keep to these rules, and one draw needn't show every extreme that they name: `doc_ids`: in each sequence the document numbers never fall; every one of the 4 documents has 1 to half of 256 tokens, and some document has exactly half of 256 tokens.
All inputs are finite; a program needn't handle non-finite values.
Results may differ from the reference program's by a relative error of at most 0.025.
Values may be sent and summed in bfloat16 or wider, within the bound.
No kernel may reach another device: no remote copies, remote signals or barrier semaphores. Data moves between devices by JAX's collectives and lax.ppermute only.
A program may use at most 256 MiB of HBM per device.

```python
import math
from functools import partial
import jax
import jax.numpy as jnp
import numpy as np
from jax import lax

D = 1152
H = 4
HD = 256
FF = 6912
SEQ = 256
DOCS = 4
SEQS = 64
TOKENS = 16384
N_DP = 64


def raised(entries, rng, source, target, parts, factor):
    def block_of(dim):
        return (jnp.arange(entries.shape[dim]) // (entries.shape[dim] // parts)).reshape((-1,) + (1,) * (entries.ndim - 1 - dim))

    first = jax.random.permutation(rng, parts)[block_of(target)]
    other_side = (block_of(target) + parts // 2) % parts
    return jnp.where((block_of(source) == first) | (block_of(source) == other_side), factor * entries, entries)


def shard_levels(rng, extent, cuts, low, high):
    gain, own = 1.0, jax.random.fold_in(rng, 6)
    for dim, parts in cuts:
        heights = jnp.exp(jax.random.uniform(jax.random.fold_in(own, dim), (parts,), jnp.float32, low / len(cuts), high / len(cuts)))
        gain = gain * jnp.repeat(heights, extent[dim] // parts).reshape([-1 if axis == dim else 1 for axis in range(len(extent))])
    return gain


def profile(count, total, most, skew):
    loads = [(1 << 20) // math.isqrt(standing ** skew) + 1 for standing in range(2, count + 1)]
    spare, holding = total - most - (count - 1), [1] * (count - 1)
    while spare > 0:
        free = [i for i in range(count - 1) if holding[i] < most]
        pool, budget = sum([loads[i] for i in free]), spare
        for i in free:
            more = min(most - holding[i], max(1, budget * loads[i] // pool), spare)
            holding[i] = holding[i] + more
            spare = spare - more
    return np.array([most] + holding)


def uneven(own_key, number_of, total, bound, slope):
    if number_of == 2:
        one = jax.random.randint(own_key, (), max(1, total - bound), min(bound, total - 1) + 1)
        return jnp.stack([one, total - one])
    sizes = jnp.asarray(profile(number_of, total, bound, slope), jnp.int32)
    twos = (number_of - 1) // 2
    source_of, taker = sizes[1:1 + 2 * twos:2], sizes[2:2 + 2 * twos:2]
    slack = jnp.minimum(source_of - 1, bound - taker)
    passed = jax.random.randint(jax.random.fold_in(own_key, 1), (twos,), 0, 1 << 20) % (slack + 1)
    sizes = sizes.at[1:1 + 2 * twos:2].set(source_of - passed).at[2:2 + 2 * twos:2].set(taker + passed)
    return sizes[jax.random.permutation(jax.random.fold_in(own_key, 2), number_of)]


def bell_draw(key, extent, spread, limit, shards=(), held_as=jnp.bfloat16):
    result = jax.random.normal(key, extent, jnp.float32) * spread
    if len(shards) > 0:
        result = shard_levels(key, extent, shards, -0.22, 0.18) * result
    return jnp.clip(result, min=-limit, max=limit).astype(held_as)


def bell_draw_with(rng, dims, width, bound, split, heavy, kind=jnp.bfloat16):
    result = width * jax.random.normal(rng, dims, jnp.float32)
    if split:
        result = result * shard_levels(rng, dims, split, -0.22, 0.18)
    return jnp.clip(raised(result, jax.random.fold_in(rng, 3), *heavy), -bound, bound).astype(kind)


def setup_inputs(seed: int = 0) -> dict:
    key_list = jax.random.split(jax.random.key(seed), 17)
    inputs = bell_draw_with(key_list[0], (TOKENS, D), 1.0, 24.0, ((0, 128),), (0, 1, 128, 5.5))
    doc_ids = jax.vmap(lambda own: jnp.searchsorted(jnp.cumsum(uneven(own, DOCS, SEQ, SEQ // 2, 0)), jnp.arange(SEQ), side="right"))(jax.random.split(key_list[1], SEQS)).reshape((SEQS, SEQ)).astype(jnp.int32)
    prenorm = jnp.clip(1.0 + 0.18 * jax.random.normal(key_list[2], (D,), jnp.float32), 0.099609375, 1.8984375).astype(jnp.bfloat16)
    query_proj = bell_draw(key_list[3], (D, H * HD), D ** -0.5, 0.1875, ((0, 64), (1, 2)))
    key_proj = bell_draw(key_list[4], (D, HD), D ** -0.5, 0.1875, ((0, 64),))
    value_proj = bell_draw(key_list[5], (D, HD), D ** -0.5, 0.1875, ((0, 64),))
    querynorm = jnp.clip(jnp.exp(math.log(2.0) - 1.3862944 * jax.random.uniform(key_list[6], (HD,), jnp.float32) ** shard_levels(key_list[6], (HD,), ((0, 64),), -0.2, 0.2)), 0.5, 2.0).astype(jnp.bfloat16)
    keynorm = jnp.clip(jnp.exp(math.log(2.0) - 1.3862944 * jax.random.uniform(key_list[7], (HD,), jnp.float32) ** shard_levels(key_list[7], (HD,), ((0, 64),), -0.2, 0.2)), 0.5, 2.0).astype(jnp.bfloat16)
    output_proj = bell_draw(key_list[8], (H * HD, D), (H * HD) ** -0.5, 0.1875, ((0, 2), (1, 64)))
    postnorm = jnp.clip(1.0 + 0.18 * jax.random.normal(key_list[9], (D,), jnp.float32), 0.099609375, 1.8984375).astype(jnp.bfloat16)
    ffnnorm = jnp.clip(1.0 + 0.18 * jax.random.normal(key_list[10], (D,), jnp.float32), 0.099609375, 1.8984375).astype(jnp.bfloat16)
    gate_proj = bell_draw(key_list[11], (D, FF), D ** -0.5, 0.1875, ((0, 64), (1, 2)))
    up_proj = bell_draw(key_list[12], (D, FF), D ** -0.5, 0.1875, ((0, 64), (1, 2)))
    down_proj = bell_draw(key_list[13], (FF, D), FF ** -0.5, 0.078125, ((0, 2), (1, 64)))
    endnorm = jnp.clip(1.0 + 0.18 * jax.random.normal(key_list[14], (D,), jnp.float32), 0.099609375, 1.8984375).astype(jnp.bfloat16)
    cotangent = bell_draw_with(key_list[15], (TOKENS, D), 1.0, 24.0, ((0, 128),), (0, 1, 128, 5.5))
    return dict(inputs=inputs, doc_ids=doc_ids, prenorm=prenorm, query_proj=query_proj, key_proj=key_proj, value_proj=value_proj, querynorm=querynorm, keynorm=keynorm, output_proj=output_proj, postnorm=postnorm, ffnnorm=ffnnorm, gate_proj=gate_proj, up_proj=up_proj, down_proj=down_proj, endnorm=endnorm, cotangent=cotangent)


epsilon = 1e-06
rope_base = 1000000.0
query_scale = 0.0625

def rms_scale(values, scales):
    mean_sq = lax.optimization_barrier(jnp.mean(values * values, axis=-1, keepdims=True))
    return values * lax.rsqrt(mean_sq + epsilon) * scales

def head_piece(cos_tab, sin_tab, factor, raw_heads, scales):
    normed = rms_scale(raw_heads, scales)
    half_width = normed.shape[-1] // 2
    first_half = normed[..., :half_width]
    second = normed[..., half_width:]
    cos_rows = cos_tab[:, None, :]
    sin_rows = sin_tab[:, None, :]
    turned = jnp.concatenate([first_half * cos_rows - second * sin_rows, second * cos_rows + first_half * sin_rows], axis=-1)
    return turned * factor

def gelu_mix(gate_in, up_in):
    return jax.nn.gelu(gate_in, approximate=True) * up_in

def matmul(left_op, right_op):
    return jnp.dot(left_op, right_op, preferred_element_type=jnp.float32)

def matmul_nt(left_op, right_op):
    return lax.dot_general(left_op, right_op, (((1,), (1,)), ((), ())), preferred_element_type=jnp.float32)

def matmul_tn(left_op, right_op):
    return lax.dot_general(left_op, right_op, (((0,), (0,)), ((), ())), preferred_element_type=jnp.float32)

def rope_tables(segment):
    seq_length = segment.shape[0]
    token_index = jnp.arange(seq_length, dtype=jnp.int32)
    same_doc = segment[:, None] == segment[None, :]
    earlier = token_index[None, :] < token_index[:, None]
    position = lax.optimization_barrier(jnp.sum(jnp.where(same_doc & earlier, 1, 0).astype(jnp.int32), axis=1)).astype(jnp.float32)
    freq_rates = jnp.exp(jnp.arange(HD // 2, dtype=jnp.float32) * (-2.0 * math.log(rope_base) / HD))
    angles = position[:, None] * freq_rates[None, :]
    allowed = same_doc & (token_index[None, :] <= token_index[:, None])
    return (jnp.cos(angles), jnp.sin(angles), allowed)

def one_sequence(x_seq, segment, d_seq, weights):
    pre_gain, query_all, key_all, value_all, qgain, kgain, out_all, post_gain, ffn_gain, gate_all, up_all, down_all, end_gain = weights
    cos_tab, sin_tab, allowed = rope_tables(segment)
    mask_rows = jnp.repeat(allowed, H, axis=0)
    resid = x_seq.astype(jnp.float32)
    normed_f, in_back = jax.vjp(rms_scale, resid, pre_gain)
    normed_in = normed_f.astype(jnp.bfloat16)
    q_raw = matmul(normed_in, query_all).reshape(SEQ, H, HD)
    k_raw = matmul(normed_in, key_all).reshape(SEQ, 1, HD)
    values_b = matmul(normed_in, value_all).astype(jnp.bfloat16)
    q_full, q_back = jax.vjp(partial(head_piece, cos_tab, sin_tab, query_scale), q_raw, qgain)
    k_full, k_back = jax.vjp(partial(head_piece, cos_tab, sin_tab, 1.0), k_raw, kgain)
    query_rows = q_full.astype(jnp.bfloat16).reshape(SEQ * H, HD)
    keys_b = k_full[:, 0, :].astype(jnp.bfloat16)
    scores = matmul_nt(query_rows, keys_b)
    exp_scores = jnp.where(mask_rows, jnp.exp(scores), 0.0)
    log_total = jnp.log(lax.optimization_barrier(jnp.sum(exp_scores, axis=1, keepdims=True)))
    probs_b = jnp.where(mask_rows, jnp.exp(scores - log_total), 0.0).astype(jnp.bfloat16)
    mixed_rows = matmul(probs_b, values_b).astype(jnp.bfloat16)
    mixed = mixed_rows.reshape(SEQ, H * HD)
    branch = matmul(mixed, out_all)
    attn_norm, attn_back = jax.vjp(rms_scale, branch, post_gain)
    hidden = resid + attn_norm
    ff_norm, ff_in_back = jax.vjp(rms_scale, hidden, ffn_gain)
    ff_input = ff_norm.astype(jnp.bfloat16)
    gate_f = matmul(ff_input, gate_all)
    up_f = matmul(ff_input, up_all)
    product, mix_back = jax.vjp(gelu_mix, gate_f, up_f)
    act = product.astype(jnp.bfloat16)
    ff_branch = matmul(act, down_all)
    end_norm, end_back = jax.vjp(rms_scale, ff_branch, end_gain)
    layer_out = (hidden + end_norm).astype(jnp.bfloat16)
    grad_out = d_seq.astype(jnp.float32)
    d_ff, grad_end = end_back(grad_out)
    d_ff_b = d_ff.astype(jnp.bfloat16)
    grad_down = matmul_tn(act, d_ff_b)
    d_act = matmul_nt(d_ff_b, down_all)
    d_gate, d_up = mix_back(d_act)
    d_gate_b = d_gate.astype(jnp.bfloat16)
    d_up_b = d_up.astype(jnp.bfloat16)
    grad_gate = matmul_tn(ff_input, d_gate_b)
    grad_up = matmul_tn(ff_input, d_up_b)
    d_ff_input = matmul_nt(d_gate_b, gate_all) + matmul_nt(d_up_b, up_all)
    d_h_part, grad_ffn = ff_in_back(d_ff_input)
    d_hidden = grad_out + d_h_part
    d_branch, grad_post = attn_back(d_hidden)
    d_branch_b = d_branch.astype(jnp.bfloat16)
    grad_outw = matmul_tn(mixed, d_branch_b)
    d_mixed = matmul_nt(d_branch_b, out_all).astype(jnp.bfloat16)
    d_mixed_rows = d_mixed.reshape(SEQ * H, HD)
    delta = lax.optimization_barrier(jnp.sum(d_mixed_rows.astype(jnp.float32) * mixed_rows.astype(jnp.float32), axis=1, keepdims=True))
    again = matmul_nt(query_rows, keys_b)
    probs_f = jnp.where(mask_rows, jnp.exp(again - log_total), 0.0)
    d_probs = matmul_nt(d_mixed_rows, values_b)
    d_scores = (probs_f * (d_probs - delta)).astype(jnp.bfloat16)
    d_queries = matmul(d_scores, keys_b).reshape(SEQ, H, HD)
    d_keys = matmul_tn(d_scores, query_rows)
    d_values = matmul_tn(probs_f.astype(jnp.bfloat16), d_mixed_rows)
    d_q_raw, grad_qgain = q_back(d_queries)
    d_k_raw, grad_kgain = k_back(d_keys[:, None, :])
    d_q_b = d_q_raw.reshape(SEQ, H * HD).astype(jnp.bfloat16)
    d_k_b = d_k_raw.reshape(SEQ, HD).astype(jnp.bfloat16)
    d_v_b = d_values.astype(jnp.bfloat16)
    grad_query = matmul_tn(normed_in, d_q_b)
    grad_key = matmul_tn(normed_in, d_k_b)
    grad_value = matmul_tn(normed_in, d_v_b)
    d_normed = matmul_nt(d_q_b, query_all) + matmul_nt(d_k_b, key_all) + matmul_nt(d_v_b, value_all)
    d_in_part, grad_pre = in_back(d_normed)
    inputs_grad = d_hidden + d_in_part
    grads = (grad_pre, grad_query, grad_key, grad_value, grad_qgain, grad_kgain, grad_outw, grad_post, grad_ffn, grad_gate, grad_up, grad_down, grad_end)
    return (layer_out, inputs_grad, grads)

def reference(inputs, doc_ids, prenorm, query_proj, key_proj, value_proj, querynorm, keynorm, output_proj, postnorm, ffnnorm, gate_proj, up_proj, down_proj, endnorm, cotangent):
    weights = (prenorm.astype(jnp.float32), query_proj, key_proj, value_proj, querynorm.astype(jnp.float32), keynorm.astype(jnp.float32), output_proj, postnorm.astype(jnp.float32), ffnnorm.astype(jnp.float32), gate_proj, up_proj, down_proj, endnorm.astype(jnp.float32))
    shapes = ((D,), (D, H * HD), (D, HD), (D, HD), (HD,), (HD,), (H * HD, D), (D,), (D,), (D, FF), (D, FF), (FF, D), (D,))
    start = tuple((jnp.zeros(shape_item, jnp.float32) for shape_item in shapes))

    def step(carry, item):
        x_seq, segment, d_seq = item
        layer_out, inputs_grad, grads = one_sequence(x_seq, segment, d_seq, weights)
        return (tuple((total + piece for total, piece in zip(carry, grads))), (layer_out, inputs_grad))
    sums, (outs, in_grads) = lax.scan(step, start, (inputs.reshape(N_DP, SEQ, D), doc_ids, cotangent.reshape(N_DP, SEQ, D)))
    return (outs.reshape(TOKENS, D), in_grads.reshape(TOKENS, D), sums[0], sums[1], sums[2], sums[3], sums[4], sums[5], sums[6], sums[7], sums[8], sums[9], sums[10], sums[11], sums[12])
```

```python
from functools import partial
import math

import jax
import jax.numpy as jnp
from jax import lax
from jax.sharding import Mesh, PartitionSpec as P

H = 4
HD = 256

epsilon = 1e-06
rope_base = 1000000.0
query_scale = 0.0625

AXES = ("x", "zh", "y", "core", "t")
SIZES = (4, 2, 4, 2, 2)
DP = ("x", "zh", "y", "core")
PLANE = ("x", "y")
ZRING = ("zh", "t")
QUAD = ("zh", "core")
LANES = 128

bf16 = jnp.bfloat16
f32 = jnp.float32


def rms_scale(values, scales):
    mean_sq = jnp.mean(values * values, axis=-1, keepdims=True)
    return values * lax.rsqrt(mean_sq + epsilon) * scales


def head_piece(cos_tab, sin_tab, factor, raw_heads, scales):
    normed = rms_scale(raw_heads, scales)
    half_width = normed.shape[-1] // 2
    first_half = normed[..., :half_width]
    second = normed[..., half_width:]
    turned = jnp.concatenate(
        [first_half * cos_tab - second * sin_tab, second * cos_tab + first_half * sin_tab],
        axis=-1,
    )
    return turned * factor


def gelu_mix(gate_in, up_in):
    return jax.nn.gelu(gate_in, approximate=True) * up_in


def matmul(left_op, right_op):
    return jnp.dot(left_op, right_op, preferred_element_type=f32)


def matmul_nt(left_op, right_op):
    return lax.dot_general(
        left_op, right_op, (((1,), (1,)), ((), ())), preferred_element_type=f32
    )


def matmul_tn(left_op, right_op):
    return lax.dot_general(
        left_op, right_op, (((0,), (0,)), ((), ())), preferred_element_type=f32
    )


def along_z(x, step):
    return lax.ppermute(x, ZRING, [(i, (i + step) % 4) for i in range(4)])


def swap(x, axis):
    return lax.ppermute(x, axis, [(0, 1), (1, 0)])


def group_gather(rows):
    near = (rows, along_z(rows, 1), along_z(rows, -1), along_z(rows, 2))
    return jnp.concatenate([*near, *(swap(b, "core") for b in near)], axis=0)


def group_scatter(part):
    n = part.shape[0] // 8
    mine, theirs = part[: 4 * n], part[4 * n :]
    both = mine.astype(f32) + swap(theirs.astype(bf16), "core").astype(f32)
    sent = both[n:].astype(bf16)
    back = (along_z(sent[:n], -1), along_z(sent[n : 2 * n], 1), along_z(sent[2 * n :], 2))
    return both[:n] + (back[0].astype(f32) + back[1].astype(f32) + back[2].astype(f32))


def sum_everywhere(x):
    for axis in ("core", "t", "zh"):
        x = x + swap(x, axis)
    for axis in ("y", "x"):
        for bit in (1, 2):
            x = x + lax.ppermute(x, axis, [(i, i ^ bit) for i in range(4)])
    return x


def mine_first(core, own, sib):
    return jnp.where(core == 0, own, sib), jnp.where(core == 0, sib, own)


def on_device(
    inputs,
    doc_ids,
    prenorm,
    query_proj,
    key_proj,
    value_proj,
    querynorm,
    keynorm,
    output_proj,
    postnorm,
    ffnnorm,
    gate_proj,
    up_proj,
    down_proj,
    endnorm,
    cotangent,
):
    core = lax.axis_index("core")
    tee = lax.axis_index("t")
    plane_index = lax.axis_index(PLANE)
    quad_index = lax.axis_index(QUAD)
    rows = prenorm.shape[0]
    head_rows = querynorm.shape[0]
    width = rows * 64
    tokens = inputs.shape[0]
    seq_length = doc_ids.shape[1]
    half_cols = HD // 2

    pos = jnp.arange(width, dtype=jnp.int32)
    p_x, p_y, p_zh, p_in = (
        pos // (16 * rows),
        pos // (4 * rows) % 4,
        pos // (2 * rows) % 2,
        pos % (2 * rows),
    )
    natural = (p_x * 8 + p_zh * 4 + p_y) * (2 * rows) + p_in
    turn = (pos[:, None] == natural[None, :]).astype(bf16)

    gains = jnp.concatenate(
        [prenorm, postnorm, ffnnorm, endnorm, querynorm, keynorm]
    )
    gains = jnp.pad(gains, (0, LANES - gains.shape[0])).reshape(1, LANES)
    gains = lax.all_gather(gains, QUAD, axis=0, tiled=True)
    gains = lax.all_gather(gains.reshape(1, 4, LANES), PLANE, axis=0, tiled=True)
    gains = gains.astype(f32)

    def width_gain(k):
        return gains[:, :, k * rows : (k + 1) * rows].reshape(width)

    def head_gain(k):
        at = 4 * rows + k * head_rows
        part = gains[:, :, at : at + head_rows].reshape(4, 4, 2, 2, head_rows)
        return part.transpose(0, 2, 1, 3, 4).reshape(HD)

    pre_gain, post_gain, ffn_gain, end_gain = (width_gain(k) for k in range(4))
    qgain, kgain = head_gain(0), head_gain(1)

    kv_pair = (
        lax.dynamic_slice_in_dim(key_proj, tee * half_cols, half_cols, axis=1),
        lax.dynamic_slice_in_dim(value_proj, tee * half_cols, half_cols, axis=1),
    )
    out_t = output_proj.T
    halves = [
        jnp.concatenate(
            [query_proj[:, c * HD : (c + 1) * HD], kv_pair[c], out_t[:, c * HD : (c + 1) * HD]],
            axis=1,
        )
        for c in range(2)
    ]
    piece = halves[0].shape[1]
    keep, give = mine_first(core, halves[0], halves[1])
    got = swap(give, "core")
    first, second = mine_first(core, keep, got)
    attn_part = jnp.stack([first, second])
    attn_part = lax.all_gather(attn_part, ZRING, axis=0, tiled=False)
    attn_part = attn_part.reshape(2, 2, 2 * rows, piece).transpose(0, 2, 1, 3)
    attn_part = attn_part.reshape(4 * rows, 2, piece)
    qkv_cols = HD + half_cols
    attn_part = jnp.concatenate(
        [
            attn_part[:, :, :qkv_cols].reshape(4 * rows, 2 * qkv_cols),
            attn_part[:, :, qkv_cols:].reshape(4 * rows, 2 * HD),
        ],
        axis=1,
    )
    attn_own = lax.all_gather(attn_part, PLANE, axis=0, tiled=True)
    qkv_own, out_own = attn_own[:, : 2 * qkv_cols], attn_own[:, 2 * qkv_cols :]
    qkv_all = jnp.concatenate([qkv_own, swap(qkv_own, "core")], axis=1)
    out_all = jnp.concatenate([out_own, swap(out_own, "core")], axis=1)

    ff_cols = gate_proj.shape[1] // 4
    ff_pad = -(-ff_cols // LANES) * LANES

    def quarters(w):
        w = w.reshape(rows, 4, ff_cols).transpose(1, 0, 2)
        return jnp.pad(w, ((0, 0), (0, 0), (0, ff_pad - ff_cols)))

    ff_part = jnp.concatenate(
        [quarters(gate_proj), quarters(up_proj), quarters(down_proj.T)], axis=2
    )
    ff_part = lax.all_to_all(ff_part, QUAD, 0, 0, tiled=True)
    ff_all = lax.all_gather(
        ff_part.reshape(4 * rows, 3 * ff_pad), PLANE, axis=0, tiled=True
    )
    gate_up_all, down_all = ff_all[:, : 2 * ff_pad], ff_all[:, 2 * ff_pad :]

    resid = matmul(inputs, turn)
    grad_out = matmul(cotangent, turn)
    segment = doc_ids[0]
    order = jnp.arange(seq_length, dtype=jnp.int32)
    own_seg = lax.dynamic_slice_in_dim(segment, tee * tokens, tokens)
    own_at = tee * tokens + jnp.arange(tokens, dtype=jnp.int32)
    peer_seg = lax.dynamic_slice_in_dim(segment, (1 - tee) * tokens, tokens)
    peer_at = (1 - tee) * tokens + jnp.arange(tokens, dtype=jnp.int32)
    position = jnp.sum(
        jnp.where(
            (own_seg[:, None] == segment[None, :]) & (order[None, :] < own_at[:, None]), 1, 0
        ).astype(jnp.int32),
        axis=1,
    ).astype(f32)
    rates = jnp.exp(jnp.arange(HD // 2, dtype=f32) * (-2.0 * math.log(rope_base) / HD))
    angles = position[:, None] * rates[None, :]
    cos_tab, sin_tab = jnp.cos(angles), jnp.sin(angles)
    key_seg = jnp.concatenate([own_seg, peer_seg])
    key_at = jnp.concatenate([own_at, peer_at])
    allowed = (own_seg[:, None] == key_seg[None, :]) & (key_at[None, :] <= own_at[:, None])
    mask_rows = jnp.tile(allowed, (H, 1))

    normed_f, in_back = jax.vjp(rms_scale, resid, pre_gain)
    normed_in = normed_f.astype(bf16)
    qkv = matmul(normed_in, qkv_all)
    q_at = [k * qkv_cols for k in range(4)]
    q_raw = jnp.stack([qkv[:, a : a + HD] for a in q_at])
    kv = [
        jnp.concatenate([qkv[:, a + HD : a + qkv_cols] for a in pair], axis=1)
        for pair in (q_at[:2], q_at[2:])
    ]
    k_raw, v_raw = mine_first(core, kv[0], kv[1])
    q_full, q_back = jax.vjp(partial(head_piece, cos_tab, sin_tab, query_scale), q_raw, qgain)
    k_full, k_back = jax.vjp(partial(head_piece, cos_tab, sin_tab, 1.0), k_raw, kgain)
    query_rows = q_full.astype(bf16).reshape(H * tokens, HD)
    kv_own = jnp.concatenate([k_full.astype(bf16), v_raw.astype(bf16)], axis=1)
    kv_both = jnp.concatenate([kv_own, swap(kv_own, "t")], axis=0)
    keys_b, values_b = kv_both[:, :HD], kv_both[:, HD:]
    scores = matmul_nt(query_rows, keys_b)
    exp_scores = jnp.where(mask_rows, jnp.exp(scores), 0.0)
    log_total = jnp.log(jnp.sum(exp_scores, axis=1, keepdims=True))
    probs_f = jnp.where(mask_rows, jnp.exp(scores - log_total), 0.0)
    probs_b = probs_f.astype(bf16)
    mixed_rows = matmul(probs_b, values_b).astype(bf16)

    def side_by_side(head_rows_of):
        return jnp.concatenate(
            [head_rows_of[h * tokens : (h + 1) * tokens] for h in range(H)], axis=1
        )

    def stacked(cols):
        return jnp.concatenate([cols[:, h * HD : (h + 1) * HD] for h in range(H)], axis=0)

    mixed = side_by_side(mixed_rows)
    branch = matmul_nt(mixed, out_all)
    attn_norm, attn_back = jax.vjp(rms_scale, branch, post_gain)
    hidden = resid + attn_norm

    ff_norm, ff_in_back = jax.vjp(rms_scale, hidden, ffn_gain)
    ff_input = group_gather(ff_norm.astype(bf16))
    gate_up = matmul(ff_input, gate_up_all)
    gate_f, up_f = gate_up[:, :ff_pad], gate_up[:, ff_pad:]
    product, mix_back = jax.vjp(gelu_mix, gate_f, up_f)
    act = product.astype(bf16)
    ff_branch = group_scatter(matmul_nt(act, down_all))
    end_norm, end_back = jax.vjp(rms_scale, ff_branch, end_gain)
    layer_out = matmul_nt((hidden + end_norm).astype(bf16), turn).astype(bf16)

    d_ff, grad_end = end_back(grad_out)
    d_ff_rows = group_gather(d_ff.astype(bf16))
    d_act = matmul(d_ff_rows, down_all)
    d_gate, d_up = mix_back(d_act)
    d_gate_up = jnp.concatenate([d_gate.astype(bf16), d_up.astype(bf16)], axis=1)
    ff_grads = jnp.concatenate(
        [matmul_tn(ff_input, d_gate_up).astype(bf16), matmul_tn(d_ff_rows, act).astype(bf16)],
        axis=1,
    )
    ff_sums = lax.psum_scatter(ff_grads, PLANE, scatter_dimension=0, tiled=True)
    ff_sums = lax.all_to_all(ff_sums.reshape(4, rows, 3 * ff_pad), QUAD, 0, 0, tiled=True)

    def joined(k):
        part = ff_sums[:, :, k * ff_pad : k * ff_pad + ff_cols]
        return part.transpose(1, 0, 2).reshape(rows, 4 * ff_cols).astype(f32)

    sent_gate, sent_up, sent_down = joined(0), joined(1), joined(2).T

    d_ff_input = group_scatter(matmul_nt(d_gate_up, gate_up_all))
    d_h_part, grad_ffn = ff_in_back(d_ff_input)
    d_hidden = grad_out + d_h_part

    d_branch, grad_post = attn_back(d_hidden)
    d_branch_b = d_branch.astype(bf16)
    out_grad = matmul_tn(d_branch_b, mixed).astype(bf16)
    d_mixed = matmul(d_branch_b, out_all).astype(bf16)
    d_mixed_rows = stacked(d_mixed)
    delta = jnp.sum(
        d_mixed_rows.astype(f32) * mixed_rows.astype(f32), axis=1, keepdims=True
    )
    d_probs = matmul_nt(d_mixed_rows, values_b)
    d_scores = (probs_f * (d_probs - delta)).astype(bf16)
    d_queries = matmul(d_scores, keys_b).reshape(H, tokens, HD)
    d_kv = jnp.concatenate(
        [matmul_tn(d_scores, query_rows), matmul_tn(probs_b, d_mixed_rows)], axis=1
    )
    d_kv = d_kv[:tokens] + swap(d_kv[tokens:].astype(bf16), "t").astype(f32)
    d_keys, d_values = d_kv[:, :HD], d_kv[:, HD:]
    d_q_raw, grad_qgain = q_back(d_queries)
    d_k_raw, grad_kgain = k_back(d_keys)
    d_own, d_sib = mine_first(core, d_k_raw.astype(bf16), d_values.astype(bf16))
    d_q_b = d_q_raw.astype(bf16)
    d_pieces = []
    for k in range(4):
        d_side = d_own if k < 2 else d_sib
        d_pieces += [d_q_b[k], d_side[:, k % 2 * half_cols : (k % 2 + 1) * half_cols]]
    d_qkv = jnp.concatenate(d_pieces, axis=1)
    qkv_grad = matmul_tn(normed_in, d_qkv).astype(bf16)
    d_normed = matmul_nt(d_qkv, qkv_all)
    d_in_part, grad_pre = in_back(d_normed)
    inputs_grad = jnp.dot(
        d_hidden + d_in_part,
        turn.T.astype(f32),
        precision=lax.Precision.HIGHEST,
        preferred_element_type=f32,
    )

    def summed(grad):
        n = grad.shape[1] // 2
        both = grad[:, :n].astype(f32) + swap(grad[:, n:], "core").astype(f32)
        return lax.psum_scatter(both.astype(bf16), PLANE, scatter_dimension=0, tiled=True)

    def over_ring(part):
        return jnp.sum(
            lax.all_to_all(part, ZRING, 0, 0, tiled=True).astype(f32), axis=0
        ).reshape(2, rows, part.shape[-1])

    def rows_of_mine(part):
        own, theirs = jnp.where(core == 0, part[0], part[1]), jnp.where(
            core == 0, part[1], part[0]
        )
        return mine_first(core, own, swap(theirs, "core"))

    out_sum = summed(out_grad).reshape(2, 2 * rows, 2, HD).transpose(0, 2, 1, 3)
    out_sum = over_ring(out_sum.reshape(4, 2 * rows, HD))
    sent_outw = jnp.concatenate(rows_of_mine(out_sum), axis=1).T

    qkv_sum = summed(qkv_grad).reshape(2, 2 * rows, 2, qkv_cols)
    q_sum = qkv_sum[..., :HD].transpose(0, 2, 1, 3)
    kv_sum = qkv_sum[..., HD:].reshape(2, 1, 2 * rows, HD)
    qkv_sum = jnp.concatenate([q_sum, jnp.broadcast_to(kv_sum, q_sum.shape)], axis=3)
    qkv_sum = over_ring(qkv_sum.reshape(4, 2 * rows, 2 * HD))
    sum_0, sum_1 = rows_of_mine(qkv_sum)
    sent_query = jnp.concatenate([sum_0[:, :HD], sum_1[:, :HD]], axis=1)
    sent_key, sent_value = sum_0[:, HD:], sum_1[:, HD:]

    gain_sums = sum_everywhere(
        jnp.concatenate([grad_pre, grad_post, grad_ffn, grad_end, grad_qgain, grad_kgain])
    )
    own_at_width = (plane_index * 4 + quad_index) * rows
    own_at_head = lax.axis_index(DP) * head_rows
    sent_pre, sent_post, sent_ffn, sent_end = (
        lax.dynamic_slice_in_dim(gain_sums, k * width + own_at_width, rows) for k in range(4)
    )
    sent_qgain, sent_kgain = (
        lax.dynamic_slice_in_dim(gain_sums, 4 * width + k * HD + own_at_head, head_rows)
        for k in range(2)
    )
    return (
        layer_out,
        inputs_grad,
        sent_pre,
        sent_query,
        sent_key,
        sent_value,
        sent_qgain,
        sent_kgain,
        sent_outw,
        sent_post,
        sent_ffn,
        sent_gate,
        sent_up,
        sent_down,
        sent_end,
    )


def solution(mesh):
    parts = Mesh(mesh.devices.reshape(SIZES), AXES)
    every = (*DP, "t")
    return jax.shard_map(
        on_device,
        mesh=parts,
        in_specs=(
            P(every, None),
            P(DP, None),
            P(DP),
            P(DP, "t"),
            P(DP, None),
            P(DP, None),
            P(DP),
            P(DP),
            P("t", DP),
            P(DP),
            P(DP),
            P(DP, "t"),
            P(DP, "t"),
            P("t", DP),
            P(DP),
            P(every, None),
        ),
        out_specs=(
            P(every, None),
            P(every, None),
            P(DP),
            P(DP, "t"),
            P(DP, None),
            P(DP, None),
            P(DP),
            P(DP),
            P("t", DP),
            P(DP),
            P(DP),
            P(DP, "t"),
            P(DP, "t"),
            P("t", DP),
            P(DP),
        ),
        check_vma=False,
    )
```

```python
from functools import partial
import math

import jax
import jax.numpy as jnp
from jax import lax
from jax.sharding import Mesh, PartitionSpec as P

H = 4
HD = 256

epsilon = 1e-06
rope_base = 1000000.0
query_scale = 0.0625

AXES = ("x", "zh", "y", "core", "t")
SIZES = (4, 2, 4, 2, 2)
DP = ("x", "zh", "y", "core")
PLANE = ("x", "y")
ZRING = ("zh", "t")
QUAD = ("zh", "core")
LANES = 128

bf16 = jnp.bfloat16
f32 = jnp.float32


def rms_scale(values, scales):
    mean_sq = jnp.mean(values * values, axis=-1, keepdims=True)
    return values * lax.rsqrt(mean_sq + epsilon) * scales


def head_piece(cos_tab, sin_tab, factor, raw_heads, scales):
    normed = rms_scale(raw_heads, scales)
    half_width = normed.shape[-1] // 2
    first_half = normed[..., :half_width]
    second = normed[..., half_width:]
    turned = jnp.concatenate(
        [first_half * cos_tab - second * sin_tab, second * cos_tab + first_half * sin_tab],
        axis=-1,
    )
    return turned * factor


def gelu_mix(gate_in, up_in):
    return jax.nn.gelu(gate_in, approximate=True) * up_in


def matmul(left_op, right_op):
    return jnp.dot(left_op, right_op, preferred_element_type=f32)


def matmul_nt(left_op, right_op):
    return lax.dot_general(
        left_op, right_op, (((1,), (1,)), ((), ())), preferred_element_type=f32
    )


def matmul_tn(left_op, right_op):
    return lax.dot_general(
        left_op, right_op, (((0,), (0,)), ((), ())), preferred_element_type=f32
    )


def along_z(x, step):
    return lax.ppermute(x, ZRING, [(i, (i + step) % 4) for i in range(4)])


def swap(x, axis):
    return lax.ppermute(x, axis, [(0, 1), (1, 0)])


def group_gather(rows):
    near = (rows, along_z(rows, 1), along_z(rows, -1), along_z(rows, 2))
    return jnp.concatenate([*near, *(swap(b, "core") for b in near)], axis=0)


def group_scatter(part):
    n = part.shape[0] // 8
    mine, theirs = part[: 4 * n], part[4 * n :]
    both = mine.astype(f32) + swap(theirs.astype(bf16), "core").astype(f32)
    sent = both[n:].astype(bf16)
    back = (along_z(sent[:n], -1), along_z(sent[n : 2 * n], 1), along_z(sent[2 * n :], 2))
    return both[:n] + (back[0].astype(f32) + back[1].astype(f32) + back[2].astype(f32))


def along(x, axis, step):
    return lax.ppermute(x, axis, [(i, (i + step) % 4) for i in range(4)])


def gather_four(x, axis, dim):
    me = lax.axis_index(axis)
    out = jnp.zeros(x.shape[:dim] + (4,) + x.shape[dim:], x.dtype)
    for step in (1, -1, 2, 0):
        block = along(x, axis, step) if step else x
        out = lax.dynamic_update_index_in_dim(out, block, (me - step) % 4, dim)
    return out


def sum_four(x, axis):
    back = [along(x[k], axis, k) for k in (1, 2, 3)]
    return x[0].astype(f32) + (
        back[0].astype(f32) + back[1].astype(f32) + back[2].astype(f32)
    )


def plane_sum(x):
    n = x.shape[0] // 16
    half = x.shape[1] // 256 * LANES
    x = x.reshape(4, 4, n, x.shape[1])
    out = []
    for part, first, second in ((x[..., :half], "y", "x"), (x[..., half:], "x", "y")):
        for axis in (first, second):
            dim = 1 if axis == "y" and axis == first else 0
            me = lax.axis_index(axis)
            blocks = [
                lax.dynamic_index_in_dim(part, (me + k) % 4, dim, keepdims=False)
                for k in range(4)
            ]
            part = sum_four([b.astype(bf16) for b in blocks], axis)
        out.append(part)
    return jnp.concatenate(out, axis=-1)


def sum_everywhere(x):
    for axis in ("core", "t", "zh"):
        x = x + swap(x, axis)
    for axis in ("y", "x"):
        for bit in (1, 2):
            x = x + lax.ppermute(x, axis, [(i, i ^ bit) for i in range(4)])
    return x


def mine_first(core, own, sib):
    return jnp.where(core == 0, own, sib), jnp.where(core == 0, sib, own)


def on_device(
    inputs,
    doc_ids,
    prenorm,
    query_proj,
    key_proj,
    value_proj,
    querynorm,
    keynorm,
    output_proj,
    postnorm,
    ffnnorm,
    gate_proj,
    up_proj,
    down_proj,
    endnorm,
    cotangent,
):
    core = lax.axis_index("core")
    tee = lax.axis_index("t")
    plane_index = lax.axis_index(PLANE)
    quad_index = lax.axis_index(QUAD)
    rows = prenorm.shape[0]
    head_rows = querynorm.shape[0]
    width = rows * 64
    tokens = inputs.shape[0]
    seq_length = doc_ids.shape[1]
    half_cols = HD // 2

    pos = lax.optimization_barrier(jnp.arange(width, dtype=jnp.int32))
    p_x, p_y, p_zh, p_in = (
        pos // (16 * rows),
        pos // (4 * rows) % 4,
        pos // (2 * rows) % 2,
        pos % (2 * rows),
    )
    natural = (p_x * 8 + p_zh * 4 + p_y) * (2 * rows) + p_in
    turn = (pos[:, None] == natural[None, :]).astype(bf16)

    kv_pair = (
        lax.dynamic_slice_in_dim(key_proj, tee * half_cols, half_cols, axis=1),
        lax.dynamic_slice_in_dim(value_proj, tee * half_cols, half_cols, axis=1),
    )
    out_t = output_proj.T
    gain_cols = jnp.stack(
        [
            prenorm,
            postnorm,
            ffnnorm,
            endnorm,
            jnp.pad(querynorm, (0, rows - head_rows)),
            jnp.pad(keynorm, (0, rows - head_rows)),
        ],
        axis=1,
    )
    gain_cols = jnp.pad(gain_cols, ((0, 0), (0, LANES - 6)))
    halves = [
        jnp.concatenate(
            [
                query_proj[:, c * HD : (c + 1) * HD],
                kv_pair[c],
                out_t[:, c * HD : (c + 1) * HD],
                gain_cols,
            ],
            axis=1,
        )
        for c in range(2)
    ]
    piece = halves[0].shape[1]
    keep, give = mine_first(core, halves[0], halves[1])
    got = swap(give, "core")
    first, second = mine_first(core, keep, got)
    attn_part = jnp.stack([first, second]).reshape(2 * rows, piece)
    z_me = lax.axis_index(ZRING)
    ring = jnp.zeros((4, 2 * rows, piece), bf16)
    for step in (1, -1, 2, 0):
        block = along_z(attn_part, step) if step else attn_part
        ring = lax.dynamic_update_index_in_dim(ring, block, (z_me - step) % 4, 0)
    ring = ring.reshape(2, 2, 2 * rows, piece)
    qkv_cols = HD + half_cols
    qkv_part = jnp.concatenate([ring[:, 0, :, :qkv_cols], ring[:, 1, :, :qkv_cols]], axis=-1)
    out_part = jnp.concatenate(
        [ring[:, 0, :, qkv_cols : qkv_cols + HD], ring[:, 1, :, qkv_cols:]], axis=-1
    )
    qkv_part = qkv_part.reshape(4 * rows, 2 * qkv_cols)
    out_part = out_part.reshape(4 * rows, 2 * HD + LANES)
    qkv_own = gather_four(gather_four(qkv_part, "y", 0), "x", 0).reshape(width, 2 * qkv_cols)
    out_own = gather_four(gather_four(out_part, "x", 0), "y", 1).reshape(width, 2 * HD + LANES)
    qkv_all = jnp.concatenate([qkv_own, swap(qkv_own, "core")], axis=1)
    gain_all = out_own[:, 2 * HD :]
    out_own = out_own[:, : 2 * HD]
    out_all = jnp.concatenate([out_own, swap(out_own, "core")], axis=1)
    pick = (
        lax.broadcasted_iota(jnp.int32, (8, LANES), 0)
        == lax.broadcasted_iota(jnp.int32, (8, LANES), 1)
    ).astype(bf16)
    gain_rows = matmul_nt(pick, gain_all)
    pre_gain, post_gain, ffn_gain, end_gain = (gain_rows[k] for k in range(4))

    def head_gain(k):
        part = gain_rows[k].reshape(4, 4, 2, 2, rows)[..., :head_rows]
        return part.transpose(0, 2, 1, 3, 4).reshape(HD)

    qgain, kgain = head_gain(4), head_gain(5)

    ff_cols = gate_proj.shape[1] // 4
    ff_pad = -(-ff_cols // LANES) * LANES

    def quarters(w):
        w = w.reshape(rows, 4, ff_cols).transpose(1, 0, 2)
        return jnp.pad(w, ((0, 0), (0, 0), (0, ff_pad - ff_cols)))

    ff_part = jnp.concatenate(
        [quarters(gate_proj), quarters(up_proj), quarters(down_proj.T)], axis=2
    )
    ff_part = lax.all_to_all(ff_part, QUAD, 0, 0, tiled=True)
    ff_all = lax.all_gather(
        ff_part.reshape(4 * rows, 3 * ff_pad), PLANE, axis=0, tiled=True
    )
    gate_up_all, down_all = ff_all[:, : 2 * ff_pad], ff_all[:, 2 * ff_pad :]

    resid = matmul(inputs, turn)
    grad_out = matmul(cotangent, turn)
    segment = doc_ids[0]
    order = jnp.arange(seq_length, dtype=jnp.int32)
    own_seg = lax.dynamic_slice_in_dim(segment, tee * tokens, tokens)
    own_at = tee * tokens + jnp.arange(tokens, dtype=jnp.int32)
    peer_seg = lax.dynamic_slice_in_dim(segment, (1 - tee) * tokens, tokens)
    peer_at = (1 - tee) * tokens + jnp.arange(tokens, dtype=jnp.int32)
    position = jnp.sum(
        jnp.where(
            (own_seg[:, None] == segment[None, :]) & (order[None, :] < own_at[:, None]), 1, 0
        ).astype(jnp.int32),
        axis=1,
    ).astype(f32)
    rates = jnp.exp(jnp.arange(HD // 2, dtype=f32) * (-2.0 * math.log(rope_base) / HD))
    angles = position[:, None] * rates[None, :]
    cos_tab, sin_tab = jnp.cos(angles), jnp.sin(angles)
    key_seg = jnp.concatenate([own_seg, peer_seg])
    key_at = jnp.concatenate([own_at, peer_at])
    allowed = (own_seg[:, None] == key_seg[None, :]) & (key_at[None, :] <= own_at[:, None])
    mask_rows = jnp.tile(allowed, (H, 1))

    normed_f, in_back = jax.vjp(rms_scale, resid, pre_gain)
    normed_in = normed_f.astype(bf16)
    qkv = matmul(normed_in, qkv_all)
    q_at = [k * qkv_cols for k in range(4)]
    q_raw = jnp.stack([qkv[:, a : a + HD] for a in q_at])
    kv = [
        jnp.concatenate([qkv[:, a + HD : a + qkv_cols] for a in pair], axis=1)
        for pair in (q_at[:2], q_at[2:])
    ]
    k_raw, v_raw = mine_first(core, kv[0], kv[1])
    q_full, q_back = jax.vjp(partial(head_piece, cos_tab, sin_tab, query_scale), q_raw, qgain)
    k_full, k_back = jax.vjp(partial(head_piece, cos_tab, sin_tab, 1.0), k_raw, kgain)
    query_rows = q_full.astype(bf16).reshape(H * tokens, HD)
    kv_own = jnp.concatenate([k_full.astype(bf16), v_raw.astype(bf16)], axis=1)
    kv_both = jnp.concatenate([kv_own, swap(kv_own, "t")], axis=0)
    keys_b, values_b = kv_both[:, :HD], kv_both[:, HD:]
    scores = matmul_nt(query_rows, keys_b)
    exp_scores = jnp.where(mask_rows, jnp.exp(scores), 0.0)
    log_total = jnp.log(jnp.sum(exp_scores, axis=1, keepdims=True))
    probs_f = jnp.where(mask_rows, jnp.exp(scores - log_total), 0.0)
    probs_b = probs_f.astype(bf16)
    mixed_rows = matmul(probs_b, values_b).astype(bf16)

    def side_by_side(head_rows_of):
        return jnp.concatenate(
            [head_rows_of[h * tokens : (h + 1) * tokens] for h in range(H)], axis=1
        )

    def stacked(cols):
        return jnp.concatenate([cols[:, h * HD : (h + 1) * HD] for h in range(H)], axis=0)

    mixed = side_by_side(mixed_rows)
    branch = matmul_nt(mixed, out_all)
    attn_norm, attn_back = jax.vjp(rms_scale, branch, post_gain)
    hidden = resid + attn_norm

    ff_norm, ff_in_back = jax.vjp(rms_scale, hidden, ffn_gain)
    ff_input = group_gather(ff_norm.astype(bf16))
    gate_up = matmul(ff_input, gate_up_all)
    gate_f, up_f = gate_up[:, :ff_pad], gate_up[:, ff_pad:]
    product, mix_back = jax.vjp(gelu_mix, gate_f, up_f)
    act = product.astype(bf16)
    ff_branch = group_scatter(matmul_nt(act, down_all))
    end_norm, end_back = jax.vjp(rms_scale, ff_branch, end_gain)
    layer_out = matmul_nt((hidden + end_norm).astype(bf16), turn).astype(bf16)

    d_ff, grad_end = end_back(grad_out)
    d_ff_rows = group_gather(d_ff.astype(bf16))
    d_act = matmul(d_ff_rows, down_all)
    d_gate, d_up = mix_back(d_act)
    d_gate_up = jnp.concatenate([d_gate.astype(bf16), d_up.astype(bf16)], axis=1)
    ff_grads = jnp.concatenate(
        [matmul_tn(ff_input, d_gate_up).astype(bf16), matmul_tn(d_ff_rows, act).astype(bf16)],
        axis=1,
    )
    d_ff_input = group_scatter(matmul_nt(d_gate_up, gate_up_all))
    d_ff_input, ff_grads = lax.optimization_barrier((d_ff_input, ff_grads))
    ff_sums = lax.psum_scatter(ff_grads, PLANE, scatter_dimension=0, tiled=True)
    ff_sums = lax.all_to_all(ff_sums.reshape(4, rows, 3 * ff_pad), QUAD, 0, 0, tiled=True)

    def joined(k):
        part = ff_sums[:, :, k * ff_pad : k * ff_pad + ff_cols]
        return part.transpose(1, 0, 2).reshape(rows, 4 * ff_cols).astype(f32)

    sent_gate, sent_up, sent_down = joined(0), joined(1), joined(2).T

    d_h_part, grad_ffn = ff_in_back(d_ff_input)
    d_hidden = grad_out + d_h_part

    d_branch, grad_post = attn_back(d_hidden)
    d_branch_b = d_branch.astype(bf16)
    out_grad = matmul_tn(d_branch_b, mixed).astype(bf16)
    d_mixed = matmul(d_branch_b, out_all).astype(bf16)
    d_mixed_rows = stacked(d_mixed)
    delta = jnp.sum(
        d_mixed_rows.astype(f32) * mixed_rows.astype(f32), axis=1, keepdims=True
    )
    d_probs = matmul_nt(d_mixed_rows, values_b)
    d_scores = (probs_f * (d_probs - delta)).astype(bf16)
    d_queries = matmul(d_scores, keys_b).reshape(H, tokens, HD)
    d_kv = jnp.concatenate(
        [matmul_tn(d_scores, query_rows), matmul_tn(probs_b, d_mixed_rows)], axis=1
    )
    d_kv = d_kv[:tokens] + swap(d_kv[tokens:].astype(bf16), "t").astype(f32)
    d_keys, d_values = d_kv[:, :HD], d_kv[:, HD:]
    d_q_raw, grad_qgain = q_back(d_queries)
    d_k_raw, grad_kgain = k_back(d_keys)
    d_own, d_sib = mine_first(core, d_k_raw.astype(bf16), d_values.astype(bf16))
    d_q_b = d_q_raw.astype(bf16)
    d_pieces = []
    for k in range(4):
        d_side = d_own if k < 2 else d_sib
        d_pieces += [d_q_b[k], d_side[:, k % 2 * half_cols : (k % 2 + 1) * half_cols]]
    d_qkv = jnp.concatenate(d_pieces, axis=1)
    qkv_grad = matmul_tn(normed_in, d_qkv).astype(bf16)
    d_normed = matmul_nt(d_qkv, qkv_all)
    d_in_part, grad_pre = in_back(d_normed)
    inputs_grad = jnp.dot(
        d_hidden + d_in_part,
        turn.T.astype(f32),
        precision=lax.Precision.HIGHEST,
        preferred_element_type=f32,
    )

    def summed(grad):
        n = grad.shape[1] // 2
        both = grad[:, :n].astype(f32) + swap(grad[:, n:], "core").astype(f32)
        return plane_sum(both.astype(bf16)).astype(bf16)

    def over_ring(part):
        return jnp.sum(
            lax.all_to_all(part, ZRING, 0, 0, tiled=True).astype(f32), axis=0
        ).reshape(2, rows, part.shape[-1])

    def rows_of_mine(part):
        own, theirs = jnp.where(core == 0, part[0], part[1]), jnp.where(
            core == 0, part[1], part[0]
        )
        return mine_first(core, own, swap(theirs, "core"))

    out_sum = summed(out_grad).reshape(2, 2 * rows, 2, HD).transpose(0, 2, 1, 3)
    out_sum = over_ring(out_sum.reshape(4, 2 * rows, HD))
    sent_outw = jnp.concatenate(rows_of_mine(out_sum), axis=1).T

    qkv_sum = summed(qkv_grad).reshape(2, 2 * rows, 2, qkv_cols)
    q_sum = qkv_sum[..., :HD].transpose(0, 2, 1, 3)
    kv_sum = qkv_sum[..., HD:].reshape(2, 1, 2 * rows, HD)
    qkv_sum = jnp.concatenate([q_sum, jnp.broadcast_to(kv_sum, q_sum.shape)], axis=3)
    qkv_sum = over_ring(qkv_sum.reshape(4, 2 * rows, 2 * HD))
    sum_0, sum_1 = rows_of_mine(qkv_sum)
    sent_query = jnp.concatenate([sum_0[:, :HD], sum_1[:, :HD]], axis=1)
    sent_key, sent_value = sum_0[:, HD:], sum_1[:, HD:]

    gain_sums = sum_everywhere(
        jnp.concatenate([grad_pre, grad_post, grad_ffn, grad_end, grad_qgain, grad_kgain])
    )
    own_at_width = (plane_index * 4 + quad_index) * rows
    own_at_head = lax.axis_index(DP) * head_rows
    sent_pre, sent_post, sent_ffn, sent_end = (
        lax.dynamic_slice_in_dim(gain_sums, k * width + own_at_width, rows) for k in range(4)
    )
    sent_qgain, sent_kgain = (
        lax.dynamic_slice_in_dim(gain_sums, 4 * width + k * HD + own_at_head, head_rows)
        for k in range(2)
    )
    return (
        layer_out,
        inputs_grad,
        sent_pre,
        sent_query,
        sent_key,
        sent_value,
        sent_qgain,
        sent_kgain,
        sent_outw,
        sent_post,
        sent_ffn,
        sent_gate,
        sent_up,
        sent_down,
        sent_end,
    )


def solution(mesh):
    parts = Mesh(mesh.devices.reshape(SIZES), AXES)
    every = (*DP, "t")
    return jax.shard_map(
        on_device,
        mesh=parts,
        in_specs=(
            P(every, None),
            P(DP, None),
            P(DP),
            P(DP, "t"),
            P(DP, None),
            P(DP, None),
            P(DP),
            P(DP),
            P("t", DP),
            P(DP),
            P(DP),
            P(DP, "t"),
            P(DP, "t"),
            P("t", DP),
            P(DP),
            P(every, None),
        ),
        out_specs=(
            P(every, None),
            P(every, None),
            P(DP),
            P(DP, "t"),
            P(DP, None),
            P(DP, None),
            P(DP),
            P(DP),
            P("t", DP),
            P(DP),
            P(DP),
            P(DP, "t"),
            P(DP, "t"),
            P("t", DP),
            P(DP),
        ),
        check_vma=False,
    )
```

```python
from functools import partial
import math

import jax
import jax.numpy as jnp
from jax import lax
from jax.sharding import Mesh, PartitionSpec as P

H = 4
HD = 256

epsilon = 1e-06
rope_base = 1000000.0
query_scale = 0.0625

AXES = ("x", "zh", "y", "core", "t")
SIZES = (4, 2, 4, 2, 2)
DP = ("x", "zh", "y", "core")
PLANE = ("x", "y")
ZRING = ("zh", "t")
QUAD = ("zh", "core")
LANES = 128

bf16 = jnp.bfloat16
f32 = jnp.float32


def rms_scale(values, scales):
    mean_sq = jnp.mean(values * values, axis=-1, keepdims=True)
    return values * lax.rsqrt(mean_sq + epsilon) * scales


def head_piece(cos_tab, sin_tab, factor, raw_heads, scales):
    normed = rms_scale(raw_heads, scales)
    half_width = normed.shape[-1] // 2
    first_half = normed[..., :half_width]
    second = normed[..., half_width:]
    turned = jnp.concatenate(
        [first_half * cos_tab - second * sin_tab, second * cos_tab + first_half * sin_tab],
        axis=-1,
    )
    return turned * factor


def gelu_mix(gate_in, up_in):
    return jax.nn.gelu(gate_in, approximate=True) * up_in


def matmul(left_op, right_op):
    return jnp.dot(left_op, right_op, preferred_element_type=f32)


def matmul_nt(left_op, right_op):
    return lax.dot_general(
        left_op, right_op, (((1,), (1,)), ((), ())), preferred_element_type=f32
    )


def matmul_tn(left_op, right_op):
    return lax.dot_general(
        left_op, right_op, (((0,), (0,)), ((), ())), preferred_element_type=f32
    )


def along_z(x, step):
    return lax.ppermute(x, ZRING, [(i, (i + step) % 4) for i in range(4)])


def swap(x, axis):
    return lax.ppermute(x, axis, [(0, 1), (1, 0)])


def group_chunks(rows, first):
    far = (along_z(rows, 2), along_z(rows, 1), along_z(rows, -1))
    home = jnp.concatenate([rows, swap(rows, "core")], axis=0)
    result = first(home)
    far = lax.optimization_barrier((*far, result[0]))[:3]
    far = [jnp.concatenate([b, swap(b, "core")], axis=0) for b in far]
    return [home, far[1], far[2], far[0]], result


def chunk_home(part, place):
    n = part.shape[0] // 2
    both = part[:n] + swap(part[n:].astype(bf16), "core").astype(f32)
    step = (0, -1, 1, 2)[place]
    return along_z(both.astype(bf16), step).astype(f32) if step else both


def along(x, axis, step):
    return lax.ppermute(x, axis, [(i, (i + step) % 4) for i in range(4)])


def quad_exchange(x):
    me = lax.axis_index(QUAD)
    got = [lax.dynamic_index_in_dim(x, me, 0, keepdims=False)] + [
        lax.ppermute(
            lax.dynamic_index_in_dim(x, me ^ k, 0, keepdims=False),
            QUAD,
            [(i, i ^ k) for i in range(4)],
        )
        for k in (1, 2, 3)
    ]
    return jnp.stack([chosen(me ^ place, got) for place in range(4)])


def chosen(which, four):
    pair = [jnp.where(which % 2 == 0, four[k], four[k + 1]) for k in (0, 2)]
    return jnp.where(which < 2, pair[0], pair[1])


def ring_sum(x):
    me = lax.axis_index(ZRING)
    blocks = [lax.dynamic_index_in_dim(x, (me + k) % 4, 0, keepdims=False) for k in range(4)]
    back = [along_z(blocks[k], k).astype(f32) for k in (1, 2, 3)]
    return blocks[0].astype(f32) + (back[0] + back[1] + back[2])


def after(x, *others):
    return lax.optimization_barrier((x, *others))[0]


def gather_four(x, axis, dim):
    me = lax.axis_index(axis)
    out = jnp.zeros(x.shape[:dim] + (4,) + x.shape[dim:], x.dtype)
    for step in (1, -1, 2, 0):
        block = along(x, axis, step) if step else x
        out = lax.dynamic_update_index_in_dim(out, block, (me - step) % 4, dim)
    return out


def sum_four(x, axis):
    back = [along(x[k], axis, k) for k in (1, 2, 3)]
    return x[0].astype(f32) + (
        back[0].astype(f32) + back[1].astype(f32) + back[2].astype(f32)
    )


def plane_sum(x):
    n = x.shape[0] // 16
    half = -(-x.shape[1] // 256) * LANES
    x = x.reshape(4, 4, n, x.shape[1])
    out = []
    for part, first, second in ((x[..., :half], "y", "x"), (x[..., half:], "x", "y")):
        for axis in (first, second):
            dim = 1 if axis == "y" and axis == first else 0
            me = lax.axis_index(axis)
            blocks = [
                lax.dynamic_index_in_dim(part, (me + k) % 4, dim, keepdims=False)
                for k in range(4)
            ]
            part = sum_four([b.astype(bf16) for b in blocks], axis)
        out.append(part)
    return jnp.concatenate(out, axis=-1)


def mine_first(core, own, sib):
    return jnp.where(core == 0, own, sib), jnp.where(core == 0, sib, own)


def on_device(
    inputs,
    doc_ids,
    prenorm,
    query_proj,
    key_proj,
    value_proj,
    querynorm,
    keynorm,
    output_proj,
    postnorm,
    ffnnorm,
    gate_proj,
    up_proj,
    down_proj,
    endnorm,
    cotangent,
):
    core = lax.axis_index("core")
    tee = lax.axis_index("t")
    rows = prenorm.shape[0]
    head_rows = querynorm.shape[0]
    width = rows * 64
    tokens = inputs.shape[0]
    seq_length = doc_ids.shape[1]
    half_cols = HD // 2

    pos = lax.optimization_barrier(jnp.arange(width, dtype=jnp.int32))
    p_x, p_y, p_zh, p_in = (
        pos // (16 * rows),
        pos // (4 * rows) % 4,
        pos // (2 * rows) % 2,
        pos % (2 * rows),
    )
    natural = (p_x * 8 + p_zh * 4 + p_y) * (2 * rows) + p_in
    turn = (pos[:, None] == natural[None, :]).astype(bf16)

    kv_pair = (
        lax.dynamic_slice_in_dim(key_proj, tee * half_cols, half_cols, axis=1),
        lax.dynamic_slice_in_dim(value_proj, tee * half_cols, half_cols, axis=1),
    )
    out_t = output_proj.T
    gain_cols = jnp.stack(
        [
            prenorm,
            postnorm,
            ffnnorm,
            endnorm,
            jnp.pad(querynorm, (0, rows - head_rows)),
            jnp.pad(keynorm, (0, rows - head_rows)),
        ],
        axis=1,
    )
    gain_cols = jnp.pad(gain_cols, ((0, 0), (0, LANES - 6)))
    halves = [
        jnp.concatenate(
            [
                query_proj[:, c * HD : (c + 1) * HD],
                kv_pair[c],
                out_t[:, c * HD : (c + 1) * HD],
                gain_cols,
            ],
            axis=1,
        )
        for c in range(2)
    ]
    piece = halves[0].shape[1]
    keep, give = mine_first(core, halves[0], halves[1])
    got = swap(give, "core")
    first, second = mine_first(core, keep, got)
    attn_part = jnp.stack([first, second]).reshape(2 * rows, piece)
    z_me = lax.axis_index(ZRING)
    blocks = [along_z(attn_part, k) if k else attn_part for k in range(4)]
    *blocks, gate_proj, up_proj, down_proj = lax.optimization_barrier(
        (*blocks, gate_proj, up_proj, down_proj)
    )
    ring = jnp.stack([chosen((z_me - place) % 4, blocks) for place in range(4)])
    ring = ring.reshape(2, 2, 2 * rows, piece)
    kv_at, o_at = HD, HD + half_cols
    g_at = o_at + HD

    def both_tees(at, stop):
        return [ring[:, k, :, at:stop] for k in range(2)]

    q_part = jnp.concatenate(both_tees(0, kv_at), axis=-1).reshape(4 * rows, 2 * HD)
    kv_part = jnp.concatenate(
        [*both_tees(kv_at, o_at), ring[:, 0, :, g_at:]], axis=-1
    ).reshape(4 * rows, HD + LANES)
    out_part = jnp.concatenate(both_tees(o_at, g_at), axis=-1).reshape(4 * rows, 2 * HD)
    q_rows, kv_rows = gather_four(q_part, "y", 0), gather_four(kv_part, "x", 0)
    out_part = after(out_part, q_rows, kv_rows)
    q_own = gather_four(q_rows, "x", 0).reshape(width, 2 * HD)
    kv_own = gather_four(kv_rows, "y", 1).reshape(width, HD + LANES)
    out_own = gather_four(gather_four(out_part, "y", 0), "x", 0).reshape(width, 2 * HD)
    qkv_own = jnp.concatenate([q_own, kv_own[:, :HD]], axis=1)
    gain_all = kv_own[:, HD:]
    qkv_all = jnp.concatenate([qkv_own, swap(qkv_own, "core")], axis=1)
    out_all = jnp.concatenate([out_own, swap(out_own, "core")], axis=1)
    pick = (
        lax.broadcasted_iota(jnp.int32, (8, LANES), 0)
        == lax.broadcasted_iota(jnp.int32, (8, LANES), 1)
    ).astype(bf16)
    gain_rows = matmul_nt(pick, gain_all)
    pre_gain, post_gain, ffn_gain, end_gain = (gain_rows[k] for k in range(4))

    def head_gain(k):
        part = gain_rows[k].reshape(4, 4, 2, 2, rows)[..., :head_rows]
        return part.transpose(0, 2, 1, 3, 4).reshape(HD)

    qgain, kgain = head_gain(4), head_gain(5)

    ff_cols = gate_proj.shape[1] // 4
    ff_pad = -(-ff_cols // LANES) * LANES

    def quarters(w):
        w = w.reshape(rows, 4, ff_cols).transpose(1, 0, 2)
        return jnp.pad(w, ((0, 0), (0, 0), (0, ff_pad - ff_cols)))

    ff_part = jnp.concatenate(
        [quarters(gate_proj), quarters(up_proj), quarters(down_proj.T)], axis=2
    )
    ff_part = quad_exchange(ff_part)
    ff_all = lax.all_gather(
        ff_part.reshape(4 * rows, 3 * ff_pad), PLANE, axis=0, tiled=True
    )
    gate_up_all, down_all = ff_all[:, : 2 * ff_pad], ff_all[:, 2 * ff_pad :]

    resid = matmul(inputs, turn)
    grad_out = matmul(cotangent, turn)
    segment = doc_ids[0]
    order = jnp.arange(seq_length, dtype=jnp.int32)
    own_seg = lax.dynamic_slice_in_dim(segment, tee * tokens, tokens)
    own_at = tee * tokens + jnp.arange(tokens, dtype=jnp.int32)
    peer_seg = lax.dynamic_slice_in_dim(segment, (1 - tee) * tokens, tokens)
    peer_at = (1 - tee) * tokens + jnp.arange(tokens, dtype=jnp.int32)
    position = jnp.sum(
        jnp.where(
            (own_seg[:, None] == segment[None, :]) & (order[None, :] < own_at[:, None]), 1, 0
        ).astype(jnp.int32),
        axis=1,
    ).astype(f32)
    rates = jnp.exp(jnp.arange(HD // 2, dtype=f32) * (-2.0 * math.log(rope_base) / HD))
    angles = position[:, None] * rates[None, :]
    cos_tab, sin_tab = jnp.cos(angles), jnp.sin(angles)
    key_seg = jnp.concatenate([own_seg, peer_seg])
    key_at = jnp.concatenate([own_at, peer_at])
    allowed = (own_seg[:, None] == key_seg[None, :]) & (key_at[None, :] <= own_at[:, None])
    mask_rows = jnp.tile(allowed, (H, 1))

    normed_f, in_back = jax.vjp(rms_scale, resid, pre_gain)
    normed_in = normed_f.astype(bf16)
    qkv = matmul(normed_in, qkv_all)
    n_qkv = 3 * HD
    q_raw = jnp.stack([qkv[:, a : a + HD] for a in (0, HD, n_qkv, n_qkv + HD)])
    k_raw, v_raw = mine_first(core, qkv[:, 2 * HD : n_qkv], qkv[:, n_qkv + 2 * HD :])
    q_full, q_back = jax.vjp(partial(head_piece, cos_tab, sin_tab, query_scale), q_raw, qgain)
    k_full, k_back = jax.vjp(partial(head_piece, cos_tab, sin_tab, 1.0), k_raw, kgain)
    query_rows = q_full.astype(bf16).reshape(H * tokens, HD)
    kv_own = jnp.concatenate([k_full.astype(bf16), v_raw.astype(bf16)], axis=1)
    kv_both = jnp.concatenate([kv_own, swap(kv_own, "t")], axis=0)
    keys_b, values_b = kv_both[:, :HD], kv_both[:, HD:]
    scores = matmul_nt(query_rows, keys_b)
    exp_scores = jnp.where(mask_rows, jnp.exp(scores), 0.0)
    log_total = jnp.log(jnp.sum(exp_scores, axis=1, keepdims=True))
    probs_f = jnp.where(mask_rows, jnp.exp(scores - log_total), 0.0)
    probs_b = probs_f.astype(bf16)
    mixed_rows = matmul(probs_b, values_b).astype(bf16)

    def side_by_side(head_rows_of):
        return jnp.concatenate(
            [head_rows_of[h * tokens : (h + 1) * tokens] for h in range(H)], axis=1
        )

    def stacked(cols):
        return jnp.concatenate([cols[:, h * HD : (h + 1) * HD] for h in range(H)], axis=0)

    mixed = side_by_side(mixed_rows)
    branch = matmul_nt(mixed, out_all)
    attn_norm, attn_back = jax.vjp(rms_scale, branch, post_gain)
    hidden = resid + attn_norm

    ff_norm, ff_in_back = jax.vjp(rms_scale, hidden, ffn_gain)

    def ff_forward(chunk):
        gate_up = matmul(chunk, gate_up_all)
        product, mix_back = jax.vjp(gelu_mix, gate_up[:, :ff_pad], gate_up[:, ff_pad:])
        act = product.astype(bf16)
        return matmul_nt(act, down_all), act, mix_back

    ff_chunks, done = group_chunks(ff_norm.astype(bf16), ff_forward)
    done = [done] + [ff_forward(chunk) for chunk in ff_chunks[1:]]
    homes = [chunk_home(done[place][0], place) for place in range(4)]
    acts, mix_backs = [d[1] for d in done], [d[2] for d in done]
    ff_branch = homes[0] + (homes[1] + homes[2] + homes[3])
    end_norm, end_back = jax.vjp(rms_scale, ff_branch, end_gain)
    layer_out = matmul_nt((hidden + end_norm).astype(bf16), turn).astype(bf16)

    d_ff, grad_end = end_back(grad_out)

    def ff_backward(chunk, place=0):
        d_gate, d_up = mix_backs[place](matmul(chunk, down_all))
        d_gate_up = jnp.concatenate([d_gate.astype(bf16), d_up.astype(bf16)], axis=1)
        return matmul_nt(d_gate_up, gate_up_all), d_gate_up

    d_ff_chunks, done = group_chunks(d_ff.astype(bf16), ff_backward)
    done = [done] + [ff_backward(d_ff_chunks[place], place) for place in (1, 2, 3)]
    homes = [chunk_home(done[place][0], place) for place in range(4)]
    d_gate_ups = [d[1] for d in done]
    ff_input, act = (
        lax.optimization_barrier(jnp.concatenate(parts, axis=0)) for parts in (ff_chunks, acts)
    )
    d_ff_rows, d_gate_up = lax.optimization_barrier(
        (
            jnp.concatenate(d_ff_chunks, axis=0),
            jnp.concatenate(d_gate_ups, axis=0),
            *(d[0] for d in done),
        )
    )[:2]
    ff_grads = jnp.concatenate(
        [matmul_tn(ff_input, d_gate_up).astype(bf16), matmul_tn(d_ff_rows, act).astype(bf16)],
        axis=1,
    )
    d_ff_input = homes[0] + (homes[1] + homes[2] + homes[3])
    d_ff_input = after(d_ff_input, ff_grads)
    ff_sums = lax.psum_scatter(ff_grads, PLANE, scatter_dimension=0, tiled=True)
    ff_sums = quad_exchange(ff_sums.reshape(4, rows, 3 * ff_pad))

    def joined(k):
        part = ff_sums[:, :, k * ff_pad : k * ff_pad + ff_cols]
        return part.transpose(1, 0, 2).reshape(rows, 4 * ff_cols).astype(f32)

    sent_gate, sent_up, sent_down = joined(0), joined(1), joined(2).T

    d_h_part, grad_ffn = ff_in_back(d_ff_input)
    d_hidden = grad_out + d_h_part

    d_branch, grad_post = attn_back(d_hidden)
    d_branch_b = d_branch.astype(bf16)
    out_grad = matmul_tn(d_branch_b, mixed).astype(bf16)
    d_mixed = matmul(d_branch_b, out_all).astype(bf16)
    d_mixed_rows = stacked(d_mixed)
    delta = jnp.sum(
        d_mixed_rows.astype(f32) * mixed_rows.astype(f32), axis=1, keepdims=True
    )
    d_probs = matmul_nt(d_mixed_rows, values_b)
    d_scores = (probs_f * (d_probs - delta)).astype(bf16)
    d_queries = matmul(d_scores, keys_b).reshape(H, tokens, HD)
    d_kv = jnp.concatenate(
        [matmul_tn(d_scores, query_rows), matmul_tn(probs_b, d_mixed_rows)], axis=1
    )
    d_kv = d_kv[:tokens] + swap(d_kv[tokens:].astype(bf16), "t").astype(f32)
    d_keys, d_values = d_kv[:, :HD], d_kv[:, HD:]
    d_q_raw, grad_qgain = q_back(d_queries)
    d_k_raw, grad_kgain = k_back(d_keys)
    d_own, d_sib = mine_first(core, d_k_raw.astype(bf16), d_values.astype(bf16))
    d_q_b = d_q_raw.astype(bf16)
    d_qkv = jnp.concatenate([d_q_b[0], d_q_b[1], d_own, d_q_b[2], d_q_b[3], d_sib], axis=1)
    qkv_grad = matmul_tn(normed_in, d_qkv).astype(bf16)
    d_normed = matmul_nt(d_qkv, qkv_all)
    d_in_part, grad_pre = in_back(d_normed)
    inputs_grad = jnp.dot(
        d_hidden + d_in_part,
        turn.T.astype(f32),
        precision=lax.Precision.HIGHEST,
        preferred_element_type=f32,
    )

    def turned_head(grad):
        grad = grad.reshape(4, 2, 4, 2, head_rows).transpose(0, 2, 1, 3, 4)
        return jnp.pad(grad, ((0, 0),) * 4 + ((0, rows - head_rows),)).reshape(width)

    gain_sets = [
        jnp.pad(jnp.stack(three), ((0, 5), (0, 0))).astype(bf16)
        for three in (
            (grad_pre, grad_post, grad_ffn),
            (grad_end, turned_head(grad_qgain), turned_head(grad_kgain)),
        )
    ]
    gain_own, gain_sib = (
        matmul_tn(g, pick).astype(bf16) for g in mine_first(core, gain_sets[0], gain_sets[1])
    )
    own_grad = jnp.concatenate([qkv_grad[:, :n_qkv], out_grad[:, : 2 * HD], gain_own], axis=1)
    sib_grad = jnp.concatenate([qkv_grad[:, n_qkv:], out_grad[:, 2 * HD :], gain_sib], axis=1)
    both = own_grad.astype(f32) + swap(sib_grad, "core").astype(f32)
    sums = plane_sum(both.astype(bf16)).astype(bf16)
    shared = (sums[:, 2 * HD : n_qkv], sums[:, n_qkv + 2 * HD :])
    for_tee = [
        jnp.concatenate(
            [
                sums[:, k * HD : (k + 1) * HD],
                sums[:, n_qkv + k * HD : n_qkv + (k + 1) * HD],
                *shared,
            ],
            axis=1,
        ).reshape(2, 1, 2 * rows, 3 * HD + LANES)
        for k in range(2)
    ]
    sums = jnp.concatenate(for_tee, axis=1).reshape(4, 2 * rows, 3 * HD + LANES)
    sums = ring_sum(sums).reshape(2, rows, 3 * HD + LANES)
    own, theirs = mine_first(core, sums[0], sums[1])
    sum_0, sum_1 = mine_first(core, own, swap(theirs, "core"))
    sent_query = jnp.concatenate([sum_0[:, :HD], sum_1[:, :HD]], axis=1)
    sent_outw = jnp.concatenate([sum_0[:, HD : 2 * HD], sum_1[:, HD : 2 * HD]], axis=1).T
    sent_key, sent_value = sum_0[:, 2 * HD : 3 * HD], sum_1[:, 2 * HD : 3 * HD]
    sent_pre, sent_post, sent_ffn = (sum_0[:, 3 * HD + k] for k in range(3))
    sent_end = sum_1[:, 3 * HD]
    sent_qgain, sent_kgain = (sum_1[:head_rows, 3 * HD + k] for k in (1, 2))
    return (
        layer_out,
        inputs_grad,
        sent_pre,
        sent_query,
        sent_key,
        sent_value,
        sent_qgain,
        sent_kgain,
        sent_outw,
        sent_post,
        sent_ffn,
        sent_gate,
        sent_up,
        sent_down,
        sent_end,
    )


def solution(mesh):
    parts = Mesh(mesh.devices.reshape(SIZES), AXES)
    every = (*DP, "t")
    return jax.shard_map(
        on_device,
        mesh=parts,
        in_specs=(
            P(every, None),
            P(DP, None),
            P(DP),
            P(DP, "t"),
            P(DP, None),
            P(DP, None),
            P(DP),
            P(DP),
            P("t", DP),
            P(DP),
            P(DP),
            P(DP, "t"),
            P(DP, "t"),
            P("t", DP),
            P(DP),
            P(every, None),
        ),
        out_specs=(
            P(every, None),
            P(every, None),
            P(DP),
            P(DP, "t"),
            P(DP, None),
            P(DP, None),
            P(DP),
            P(DP),
            P("t", DP),
            P(DP),
            P(DP),
            P(DP, "t"),
            P(DP, "t"),
            P("t", DP),
            P(DP),
        ),
        check_vma=False,
    )
```

```python
from functools import partial
import math

import jax
import jax.numpy as jnp
from jax import lax
from jax.experimental.layout import Layout, with_layout_constraint
from jax.sharding import Mesh, PartitionSpec as P

H = 4
HD = 256

epsilon = 1e-06
rope_base = 1000000.0
query_scale = 0.0625

AXES = ("x", "zh", "y", "core", "t")
SIZES = (4, 2, 4, 2, 2)
DP = ("x", "zh", "y", "core")
PLANE = ("x", "y")
ZRING = ("zh", "t")
QUAD = ("zh", "core")
LANES = 128

bf16 = jnp.bfloat16
f32 = jnp.float32


def rms_scale(values, scales):
    mean_sq = jnp.mean(values * values, axis=-1, keepdims=True)
    return values * lax.rsqrt(mean_sq + epsilon) * scales


def head_piece(cos_tab, sin_tab, factor, raw_heads, scales):
    normed = rms_scale(raw_heads, scales)
    half_width = normed.shape[-1] // 2
    first_half = normed[..., :half_width]
    second = normed[..., half_width:]
    turned = jnp.concatenate(
        [first_half * cos_tab - second * sin_tab, second * cos_tab + first_half * sin_tab],
        axis=-1,
    )
    return turned * factor


def gelu_mix(gate_in, up_in):
    return jax.nn.gelu(gate_in, approximate=True) * up_in


def matmul(left_op, right_op):
    return jnp.dot(left_op, right_op, preferred_element_type=f32)


def matmul_nt(left_op, right_op):
    return lax.dot_general(
        left_op, right_op, (((1,), (1,)), ((), ())), preferred_element_type=f32
    )


def rows_first(x):
    return with_layout_constraint(x, Layout(major_to_minor=(0, 1)))


def matmul_tn(left_op, right_op):
    return lax.dot_general(
        left_op, right_op, (((0,), (0,)), ((), ())), preferred_element_type=f32
    )


def along_z(x, step):
    return lax.ppermute(x, ZRING, [(i, (i + step) % 4) for i in range(4)])


def swap(x, axis):
    return lax.ppermute(x, axis, [(0, 1), (1, 0)])


def group_chunks(rows):
    far = along_z(rows, 2)
    near = (rows, along_z(rows, 1), along_z(rows, -1), far)
    return [jnp.concatenate([b, swap(b, "core")], axis=0) for b in near]


def chunk_home(part, place):
    n = part.shape[0] // 2
    both = part[:n] + swap(part[n:].astype(bf16), "core").astype(f32)
    step = (0, -1, 1, 2)[place]
    return along_z(both.astype(bf16), step).astype(f32) if step else both


def along(x, axis, step):
    return lax.ppermute(x, axis, [(i, (i + step) % 4) for i in range(4)])


def quad_exchange(x):
    me = lax.axis_index(QUAD)
    got = [lax.dynamic_index_in_dim(x, me, 0, keepdims=False)] + [
        lax.ppermute(
            lax.dynamic_index_in_dim(x, me ^ k, 0, keepdims=False),
            QUAD,
            [(i, i ^ k) for i in range(4)],
        )
        for k in (1, 2, 3)
    ]
    return jnp.stack([chosen(me ^ place, got) for place in range(4)])


def chosen(which, four):
    pair = [jnp.where(which % 2 == 0, four[k], four[k + 1]) for k in (0, 2)]
    return jnp.where(which < 2, pair[0], pair[1])


def ring_sum(x):
    me = lax.axis_index(ZRING)
    blocks = [lax.dynamic_index_in_dim(x, (me + k) % 4, 0, keepdims=False) for k in range(4)]
    back = [along_z(blocks[k], k).astype(f32) for k in (1, 2, 3)]
    return blocks[0].astype(f32) + (back[0] + back[1] + back[2])


def after(x, *others):
    return lax.optimization_barrier((x, *others))[0]


def gather_four(x, axis, dim):
    me = lax.axis_index(axis)
    out = jnp.zeros(x.shape[:dim] + (4,) + x.shape[dim:], x.dtype)
    for step in (1, -1, 2, 0):
        block = along(x, axis, step) if step else x
        out = lax.dynamic_update_index_in_dim(out, block, (me - step) % 4, dim)
    return out


def sum_four(x, axis):
    back = [along(x[k], axis, k) for k in (1, 2, 3)]
    return x[0].astype(f32) + (
        back[0].astype(f32) + back[1].astype(f32) + back[2].astype(f32)
    )


def plane_sum(x):
    n = x.shape[0] // 16
    half = -(-x.shape[1] // 256) * LANES
    x = x.reshape(4, 4, n, x.shape[1])
    out = []
    for part, first, second in ((x[..., :half], "y", "x"), (x[..., half:], "x", "y")):
        for axis in (first, second):
            dim = 1 if axis == "y" and axis == first else 0
            me = lax.axis_index(axis)
            blocks = [
                lax.dynamic_index_in_dim(part, (me + k) % 4, dim, keepdims=False)
                for k in range(4)
            ]
            part = sum_four([b.astype(bf16) for b in blocks], axis)
        out.append(part)
    return jnp.concatenate(out, axis=-1)


def mine_first(core, own, sib):
    return jnp.where(core == 0, own, sib), jnp.where(core == 0, sib, own)


def on_device(
    inputs,
    doc_ids,
    prenorm,
    query_proj,
    key_proj,
    value_proj,
    querynorm,
    keynorm,
    output_proj,
    postnorm,
    ffnnorm,
    gate_proj,
    up_proj,
    down_proj,
    endnorm,
    cotangent,
):
    core = lax.axis_index("core")
    tee = lax.axis_index("t")
    rows = prenorm.shape[0]
    head_rows = querynorm.shape[0]
    width = rows * 64
    tokens = inputs.shape[0]
    seq_length = doc_ids.shape[1]
    half_cols = HD // 2

    pos = lax.optimization_barrier(jnp.arange(width, dtype=jnp.int32))
    p_x, p_y, p_zh, p_in = (
        pos // (16 * rows),
        pos // (4 * rows) % 4,
        pos // (2 * rows) % 2,
        pos % (2 * rows),
    )
    natural = (p_x * 8 + p_zh * 4 + p_y) * (2 * rows) + p_in
    turn = (pos[:, None] == natural[None, :]).astype(bf16)

    kv_pair = (
        lax.dynamic_slice_in_dim(key_proj, tee * half_cols, half_cols, axis=1),
        lax.dynamic_slice_in_dim(value_proj, tee * half_cols, half_cols, axis=1),
    )
    out_t = output_proj.T
    gain_cols = jnp.stack(
        [
            prenorm,
            postnorm,
            ffnnorm,
            endnorm,
            jnp.pad(querynorm, (0, rows - head_rows)),
            jnp.pad(keynorm, (0, rows - head_rows)),
        ],
        axis=1,
    )
    gain_cols = jnp.pad(gain_cols, ((0, 0), (0, LANES - 6)))
    halves = [
        jnp.concatenate(
            [
                query_proj[:, c * HD : (c + 1) * HD],
                kv_pair[c],
                gain_cols,
                out_t[:, c * HD : (c + 1) * HD],
            ],
            axis=1,
        )
        for c in range(2)
    ]
    piece = halves[0].shape[1]
    keep, give = mine_first(core, halves[0], halves[1])
    got = swap(give, "core")
    first, second = mine_first(core, keep, got)
    attn_part = jnp.stack([first, second]).reshape(2 * rows, piece)
    attn_part, gate_proj, up_proj, down_proj = lax.optimization_barrier(
        (attn_part, gate_proj, up_proj, down_proj)
    )
    ff_cols = gate_proj.shape[1] // 4
    ff_pad = -(-ff_cols // LANES) * LANES

    def quarters(w):
        w = w.reshape(rows, 4, ff_cols).transpose(1, 0, 2)
        return jnp.pad(w, ((0, 0), (0, 0), (0, ff_pad - ff_cols)))

    ff_part = jnp.concatenate(
        [quarters(gate_proj), quarters(up_proj), quarters(down_proj.T)], axis=2
    )
    ff_part = quad_exchange(ff_part)
    both_z = jnp.stack(mine_first(lax.axis_index("zh"), attn_part, swap(attn_part, "zh")))
    attn_part = both_z.reshape(4 * rows, piece)
    o_at = piece - HD
    q_rows = gather_four(attn_part[:, :HD], "y", 0)
    kv_rows = gather_four(attn_part[:, HD:o_at], "x", 0)
    q_rows, kv_rows, ff_part = lax.optimization_barrier(
        (q_rows, kv_rows, ff_part.reshape(4 * rows, 3 * ff_pad))
    )
    out_part = after(attn_part[:, o_at:], q_rows, kv_rows)
    q_half = gather_four(q_rows, "x", 0).reshape(width, HD)
    kv_half = gather_four(kv_rows, "y", 1).reshape(width, o_at - HD)
    gain_all = kv_half[:, half_cols:]
    qkv_half = jnp.concatenate([q_half, kv_half[:, :half_cols]], axis=1)
    qkv_two = mine_first(tee, qkv_half, swap(qkv_half, "t"))
    out_half = gather_four(gather_four(out_part, "y", 0), "x", 0).reshape(width, HD)
    out_two = mine_first(tee, out_half, swap(out_half, "t"))
    qkv_own = jnp.concatenate(
        [
            qkv_two[0][:, :HD],
            qkv_two[1][:, :HD],
            qkv_two[0][:, HD:],
            qkv_two[1][:, HD:],
        ],
        axis=1,
    )
    out_own = jnp.concatenate([out_two[0], out_two[1]], axis=1)
    qkv_all = jnp.concatenate([qkv_own, swap(qkv_own, "core")], axis=1)
    out_all = jnp.concatenate([out_own, swap(out_own, "core")], axis=1)
    pick = (
        lax.broadcasted_iota(jnp.int32, (8, LANES), 0)
        == lax.broadcasted_iota(jnp.int32, (8, LANES), 1)
    ).astype(bf16)
    gain_rows = matmul_nt(pick, gain_all)
    pre_gain, post_gain, ffn_gain, end_gain = (gain_rows[k] for k in range(4))

    def head_gain(k):
        part = gain_rows[k].reshape(4, 4, 2, 2, rows)[..., :head_rows]
        return part.transpose(0, 2, 1, 3, 4).reshape(HD)

    qgain, kgain = head_gain(4), head_gain(5)

    ff_all = lax.all_gather(
        ff_part, PLANE, axis=0, tiled=True
    )
    gate_all, up_all, down_all = (
        ff_all[:, k * ff_pad : (k + 1) * ff_pad] for k in range(3)
    )

    resid = matmul(inputs, turn)
    grad_out = matmul(cotangent, turn)
    segment = doc_ids[0]
    order = jnp.arange(seq_length, dtype=jnp.int32)
    own_seg = lax.dynamic_slice_in_dim(segment, tee * tokens, tokens)
    own_at = tee * tokens + jnp.arange(tokens, dtype=jnp.int32)
    peer_seg = lax.dynamic_slice_in_dim(segment, (1 - tee) * tokens, tokens)
    peer_at = (1 - tee) * tokens + jnp.arange(tokens, dtype=jnp.int32)
    position = jnp.sum(
        jnp.where(
            (own_seg[:, None] == segment[None, :]) & (order[None, :] < own_at[:, None]), 1, 0
        ).astype(jnp.int32),
        axis=1,
    ).astype(f32)
    rates = jnp.exp(jnp.arange(HD // 2, dtype=f32) * (-2.0 * math.log(rope_base) / HD))
    angles = position[:, None] * rates[None, :]
    cos_tab, sin_tab = jnp.cos(angles), jnp.sin(angles)
    key_seg = jnp.concatenate([own_seg, peer_seg])
    key_at = jnp.concatenate([own_at, peer_at])
    allowed = (own_seg[:, None] == key_seg[None, :]) & (key_at[None, :] <= own_at[:, None])
    mask_rows = jnp.tile(allowed, (H, 1))

    normed_f, in_back = jax.vjp(rms_scale, resid, pre_gain)
    normed_in = normed_f.astype(bf16)
    qkv = matmul(normed_in, qkv_all)
    n_qkv = 3 * HD
    q_raw = jnp.stack([qkv[:, a : a + HD] for a in (0, HD, n_qkv, n_qkv + HD)])
    k_raw, v_raw = mine_first(core, qkv[:, 2 * HD : n_qkv], qkv[:, n_qkv + 2 * HD :])
    q_full, q_back = jax.vjp(partial(head_piece, cos_tab, sin_tab, query_scale), q_raw, qgain)
    k_full, k_back = jax.vjp(partial(head_piece, cos_tab, sin_tab, 1.0), k_raw, kgain)
    query_rows = q_full.astype(bf16).reshape(H * tokens, HD)
    kv_own = jnp.concatenate([k_full.astype(bf16), v_raw.astype(bf16)], axis=1)
    kv_both = jnp.concatenate([kv_own, swap(kv_own, "t")], axis=0)
    keys_b, values_b = kv_both[:, :HD], kv_both[:, HD:]
    scores = matmul_nt(query_rows, keys_b)
    exp_scores = jnp.where(mask_rows, jnp.exp(scores), 0.0)
    log_total = jnp.log(jnp.sum(exp_scores, axis=1, keepdims=True))
    probs_f = jnp.where(mask_rows, jnp.exp(scores - log_total), 0.0)
    probs_b = probs_f.astype(bf16)
    mixed_rows = matmul(probs_b, values_b).astype(bf16)

    def side_by_side(head_rows_of):
        return jnp.concatenate(
            [head_rows_of[h * tokens : (h + 1) * tokens] for h in range(H)], axis=1
        )

    def stacked(cols):
        return jnp.concatenate([cols[:, h * HD : (h + 1) * HD] for h in range(H)], axis=0)

    mixed = side_by_side(mixed_rows)
    branch = matmul_nt(mixed, out_all)
    attn_norm, attn_back = jax.vjp(rms_scale, branch, post_gain)
    hidden = resid + attn_norm

    ff_norm, ff_in_back = jax.vjp(rms_scale, hidden, ffn_gain)

    def ff_forward(chunk):
        product, mix_back = jax.vjp(gelu_mix, matmul(chunk, gate_all), matmul(chunk, up_all))
        act = product.astype(bf16)
        return rows_first(matmul_nt(act, down_all)), act, mix_back

    ff_chunks = group_chunks(ff_norm.astype(bf16))
    done = [ff_forward(chunk) for chunk in ff_chunks]
    homes = [chunk_home(done[place][0], place) for place in range(4)]
    acts, mix_backs = [d[1] for d in done], [d[2] for d in done]
    ff_branch = homes[0] + (homes[1] + homes[2] + homes[3])
    end_norm, end_back = jax.vjp(rms_scale, ff_branch, end_gain)
    layer_out = matmul_nt((hidden + end_norm).astype(bf16), turn).astype(bf16)

    d_ff, grad_end = end_back(grad_out)

    def ff_backward(chunk, place):
        d_gate, d_up = mix_backs[place](matmul(chunk, down_all))
        d_gate, d_up = d_gate.astype(bf16), d_up.astype(bf16)
        d_chunk = matmul_nt(d_gate, gate_all) + matmul_nt(d_up, up_all)
        return rows_first(d_chunk), d_gate, d_up

    d_ff_chunks = group_chunks(d_ff.astype(bf16))
    done = [ff_backward(d_ff_chunks[place], place) for place in range(4)]
    homes = [chunk_home(done[place][0], place) for place in range(4)]
    ff_input, act, d_ff_rows, d_gate, d_up = (
        jnp.concatenate(lax.optimization_barrier(parts), axis=0)
        for parts in (
            ff_chunks,
            acts,
            d_ff_chunks,
            [d[1] for d in done],
            [d[2] for d in done],
        )
    )
    ff_input, act, d_ff_rows, d_gate, d_up, *_ = lax.optimization_barrier(
        (ff_input, act, d_ff_rows, d_gate, d_up, *(d[0] for d in done))
    )
    ff_grads = jnp.concatenate(
        [
            matmul_tn(ff_input, d_gate).astype(bf16),
            matmul_tn(ff_input, d_up).astype(bf16),
            matmul_tn(d_ff_rows, act).astype(bf16),
        ],
        axis=1,
    )
    d_ff_input = homes[0] + (homes[1] + homes[2] + homes[3])
    d_ff_input = after(d_ff_input, ff_grads)
    ff_sums = lax.psum_scatter(rows_first(ff_grads), PLANE, scatter_dimension=0, tiled=True)
    ff_sums = quad_exchange(ff_sums.reshape(4, rows, 3 * ff_pad))

    def joined(k):
        part = ff_sums[:, :, k * ff_pad : k * ff_pad + ff_cols]
        return part.transpose(1, 0, 2).reshape(rows, 4 * ff_cols).astype(f32)

    sent_gate, sent_up, sent_down = joined(0), joined(1), joined(2).T

    d_h_part, grad_ffn = ff_in_back(d_ff_input)
    d_hidden = grad_out + d_h_part

    d_branch, grad_post = attn_back(d_hidden)
    d_branch_b = d_branch.astype(bf16)
    out_grad = matmul_tn(d_branch_b, mixed).astype(bf16)
    d_mixed = matmul(d_branch_b, out_all).astype(bf16)
    d_mixed_rows = stacked(d_mixed)
    delta = jnp.sum(
        d_mixed_rows.astype(f32) * mixed_rows.astype(f32), axis=1, keepdims=True
    )
    d_probs = matmul_nt(d_mixed_rows, values_b)
    d_scores = (probs_f * (d_probs - delta)).astype(bf16)
    d_queries = matmul(d_scores, keys_b).reshape(H, tokens, HD)
    d_kv = jnp.concatenate(
        [matmul_tn(d_scores, query_rows), matmul_tn(probs_b, d_mixed_rows)], axis=1
    )
    d_kv = d_kv[:tokens] + swap(d_kv[tokens:].astype(bf16), "t").astype(f32)
    d_keys, d_values = d_kv[:, :HD], d_kv[:, HD:]
    d_q_raw, grad_qgain = q_back(d_queries)
    d_k_raw, grad_kgain = k_back(d_keys)
    d_own, d_sib = mine_first(core, d_k_raw.astype(bf16), d_values.astype(bf16))
    d_q_b = d_q_raw.astype(bf16)
    d_qkv = jnp.concatenate([d_q_b[0], d_q_b[1], d_own, d_q_b[2], d_q_b[3], d_sib], axis=1)
    qkv_grad = matmul_tn(normed_in, d_qkv).astype(bf16)
    d_normed = matmul_nt(d_qkv, qkv_all)
    d_in_part, grad_pre = in_back(d_normed)
    inputs_grad = jnp.dot(
        d_hidden + d_in_part,
        turn.T.astype(f32),
        precision=lax.Precision.HIGHEST,
        preferred_element_type=f32,
    )

    def turned_head(grad):
        grad = grad.reshape(4, 2, 4, 2, head_rows).transpose(0, 2, 1, 3, 4)
        return jnp.pad(grad, ((0, 0),) * 4 + ((0, rows - head_rows),)).reshape(width)

    gain_sets = [
        jnp.pad(jnp.stack(three), ((0, 5), (0, 0))).astype(bf16)
        for three in (
            (grad_pre, grad_post, grad_ffn),
            (grad_end, turned_head(grad_qgain), turned_head(grad_kgain)),
        )
    ]
    gain_own, gain_sib = (
        matmul_tn(g, pick).astype(bf16) for g in mine_first(core, gain_sets[0], gain_sets[1])
    )
    own_grad = jnp.concatenate([qkv_grad[:, :n_qkv], out_grad[:, : 2 * HD], gain_own], axis=1)
    sib_grad = jnp.concatenate([qkv_grad[:, n_qkv:], out_grad[:, 2 * HD :], gain_sib], axis=1)
    both = own_grad.astype(f32) + swap(sib_grad, "core").astype(f32)
    sums = plane_sum(both.astype(bf16)).astype(bf16)
    shared = (sums[:, 2 * HD : n_qkv], sums[:, n_qkv + 2 * HD :])
    for_tee = [
        jnp.concatenate(
            [
                sums[:, k * HD : (k + 1) * HD],
                sums[:, n_qkv + k * HD : n_qkv + (k + 1) * HD],
                *shared,
            ],
            axis=1,
        ).reshape(2, 1, 2 * rows, 3 * HD + LANES)
        for k in range(2)
    ]
    sums = jnp.concatenate(for_tee, axis=1).reshape(4, 2 * rows, 3 * HD + LANES)
    sums = ring_sum(sums).reshape(2, rows, 3 * HD + LANES)
    own, theirs = mine_first(core, sums[0], sums[1])
    sum_0, sum_1 = mine_first(core, own, swap(theirs, "core"))
    sent_query = jnp.concatenate([sum_0[:, :HD], sum_1[:, :HD]], axis=1)
    sent_outw = jnp.concatenate([sum_0[:, HD : 2 * HD], sum_1[:, HD : 2 * HD]], axis=1).T
    sent_key, sent_value = sum_0[:, 2 * HD : 3 * HD], sum_1[:, 2 * HD : 3 * HD]
    sent_pre, sent_post, sent_ffn = (sum_0[:, 3 * HD + k] for k in range(3))
    sent_end = sum_1[:, 3 * HD]
    sent_qgain, sent_kgain = (sum_1[:head_rows, 3 * HD + k] for k in (1, 2))
    return (
        layer_out,
        inputs_grad,
        sent_pre,
        sent_query,
        sent_key,
        sent_value,
        sent_qgain,
        sent_kgain,
        sent_outw,
        sent_post,
        sent_ffn,
        sent_gate,
        sent_up,
        sent_down,
        sent_end,
    )


def solution(mesh):
    parts = Mesh(mesh.devices.reshape(SIZES), AXES)
    every = (*DP, "t")
    return jax.shard_map(
        on_device,
        mesh=parts,
        in_specs=(
            P(every, None),
            P(DP, None),
            P(DP),
            P(DP, "t"),
            P(DP, None),
            P(DP, None),
            P(DP),
            P(DP),
            P("t", DP),
            P(DP),
            P(DP),
            P(DP, "t"),
            P(DP, "t"),
            P("t", DP),
            P(DP),
            P(every, None),
        ),
        out_specs=(
            P(every, None),
            P(every, None),
            P(DP),
            P(DP, "t"),
            P(DP, None),
            P(DP, None),
            P(DP),
            P(DP),
            P("t", DP),
            P(DP),
            P(DP),
            P(DP, "t"),
            P(DP, "t"),
            P("t", DP),
            P(DP),
        ),
        check_vma=False,
    )
```

```python
from functools import partial
import math

import jax
import jax.numpy as jnp
from jax import lax
from jax.experimental.layout import Layout, with_layout_constraint
from jax.sharding import Mesh, PartitionSpec as P

H = 4
HD = 256

epsilon = 1e-06
rope_base = 1000000.0
query_scale = 0.0625

AXES = ("x", "zh", "y", "core", "t")
SIZES = (4, 2, 4, 2, 2)
DP = ("x", "zh", "y", "core")
PLANE = ("x", "y")
ZRING = ("zh", "t")
QUAD = ("zh", "core")
LANES = 128

bf16 = jnp.bfloat16
f32 = jnp.float32


def rms_scale(values, scales):
    mean_sq = jnp.mean(values * values, axis=-1, keepdims=True)
    return values * lax.rsqrt(mean_sq + epsilon) * scales


def head_piece(cos_tab, sin_tab, factor, raw_heads, scales):
    normed = rms_scale(raw_heads, scales)
    half_width = normed.shape[-1] // 2
    first_half = normed[..., :half_width]
    second = normed[..., half_width:]
    turned = jnp.concatenate(
        [first_half * cos_tab - second * sin_tab, second * cos_tab + first_half * sin_tab],
        axis=-1,
    )
    return turned * factor


def gelu_mix(gate_in, up_in):
    return jax.nn.gelu(gate_in, approximate=True) * up_in


def matmul(left_op, right_op):
    return jnp.dot(left_op, right_op, preferred_element_type=f32)


def matmul_nt(left_op, right_op):
    return lax.dot_general(
        left_op, right_op, (((1,), (1,)), ((), ())), preferred_element_type=f32
    )


def rows_first(x):
    return with_layout_constraint(x, Layout(major_to_minor=(0, 1)))


def matmul_tn(left_op, right_op):
    return lax.dot_general(
        left_op, right_op, (((0,), (0,)), ((), ())), preferred_element_type=f32
    )


def along_z(x, step):
    return lax.ppermute(x, ZRING, [(i, (i + step) % 4) for i in range(4)])


def swap(x, axis):
    return lax.ppermute(x, axis, [(0, 1), (1, 0)])


def group_chunks(rows):
    far = along_z(rows, 2)
    near = (rows, along_z(rows, 1), along_z(rows, -1), far)
    return [jnp.concatenate([b, swap(b, "core")], axis=0) for b in near]


def chunk_home(part, place):
    n = part.shape[0] // 2
    both = part[:n] + swap(part[n:].astype(bf16), "core").astype(f32)
    step = (0, -1, 1, 2)[place]
    return along_z(both.astype(bf16), step).astype(f32) if step else both


def along(x, axis, step):
    return lax.ppermute(x, axis, [(i, (i + step) % 4) for i in range(4)])


def quad_exchange(x):
    me = lax.axis_index(QUAD)
    got = [lax.dynamic_index_in_dim(x, me, 0, keepdims=False)] + [
        lax.ppermute(
            lax.dynamic_index_in_dim(x, me ^ k, 0, keepdims=False),
            QUAD,
            [(i, i ^ k) for i in range(4)],
        )
        for k in (1, 2, 3)
    ]
    return jnp.stack([chosen(me ^ place, got) for place in range(4)])


def chosen(which, four):
    pair = [jnp.where(which % 2 == 0, four[k], four[k + 1]) for k in (0, 2)]
    return jnp.where(which < 2, pair[0], pair[1])


def ring_sum(x):
    me = lax.axis_index(ZRING)
    blocks = [lax.dynamic_index_in_dim(x, (me + k) % 4, 0, keepdims=False) for k in range(4)]
    back = [along_z(blocks[k], k).astype(f32) for k in (1, 2, 3)]
    return blocks[0].astype(f32) + (back[0] + back[1] + back[2])


def after(x, *others):
    return lax.optimization_barrier((x, *others))[0]


def gather_four(x, axis, dim):
    me = lax.axis_index(axis)
    out = jnp.zeros(x.shape[:dim] + (4,) + x.shape[dim:], x.dtype)
    for step in (1, -1, 2, 0):
        block = along(x, axis, step) if step else x
        out = lax.dynamic_update_index_in_dim(out, block, (me - step) % 4, dim)
    return out


def sum_four(x, axis):
    back = [along(x[k], axis, k) for k in (1, 2, 3)]
    return x[0].astype(f32) + (
        back[0].astype(f32) + back[1].astype(f32) + back[2].astype(f32)
    )


def plane_sum(x, first, second):
    x = x.reshape(4, 4, x.shape[0] // 16, x.shape[1])
    for axis in (first, second):
        dim = 1 if axis == "y" and axis == first else 0
        me = lax.axis_index(axis)
        blocks = [
            lax.dynamic_index_in_dim(x, (me + k) % 4, dim, keepdims=False) for k in range(4)
        ]
        x = sum_four([b.astype(bf16) for b in blocks], axis)
    return x.astype(bf16)


def mine_first(core, own, sib):
    return jnp.where(core == 0, own, sib), jnp.where(core == 0, sib, own)


def on_device(
    inputs,
    doc_ids,
    prenorm,
    query_proj,
    key_proj,
    value_proj,
    querynorm,
    keynorm,
    output_proj,
    postnorm,
    ffnnorm,
    gate_proj,
    up_proj,
    down_proj,
    endnorm,
    cotangent,
):
    core = lax.axis_index("core")
    tee = lax.axis_index("t")
    rows = prenorm.shape[0]
    head_rows = querynorm.shape[0]
    width = rows * 64
    tokens = inputs.shape[0]
    seq_length = doc_ids.shape[1]
    half_cols = HD // 2

    pos = lax.optimization_barrier(jnp.arange(width, dtype=jnp.int32))
    p_x, p_y, p_zh, p_in = (
        pos // (16 * rows),
        pos // (4 * rows) % 4,
        pos // (2 * rows) % 2,
        pos % (2 * rows),
    )
    natural = (p_x * 8 + p_zh * 4 + p_y) * (2 * rows) + p_in
    turn = (pos[:, None] == natural[None, :]).astype(bf16)

    kv_pair = (
        lax.dynamic_slice_in_dim(key_proj, tee * half_cols, half_cols, axis=1),
        lax.dynamic_slice_in_dim(value_proj, tee * half_cols, half_cols, axis=1),
    )
    out_t = output_proj.T
    gain_cols = jnp.stack(
        [
            prenorm,
            postnorm,
            ffnnorm,
            endnorm,
            jnp.pad(querynorm, (0, rows - head_rows)),
            jnp.pad(keynorm, (0, rows - head_rows)),
        ],
        axis=1,
    )
    gain_cols = jnp.pad(gain_cols, ((0, 0), (0, LANES - 6)))
    halves = [
        jnp.concatenate(
            [
                query_proj[:, c * HD : (c + 1) * HD],
                kv_pair[c],
                gain_cols,
                out_t[:, c * HD : (c + 1) * HD],
            ],
            axis=1,
        )
        for c in range(2)
    ]
    piece = halves[0].shape[1]
    keep, give = mine_first(core, halves[0], halves[1])
    got = swap(give, "core")
    first, second = mine_first(core, keep, got)
    attn_part = jnp.stack([first, second]).reshape(2 * rows, piece)
    attn_part, gate_proj, up_proj, down_proj = lax.optimization_barrier(
        (attn_part, gate_proj, up_proj, down_proj)
    )
    ff_cols = gate_proj.shape[1] // 4
    ff_pad = -(-ff_cols // LANES) * LANES

    def quarters(w):
        w = w.reshape(rows, 4, ff_cols).transpose(1, 0, 2)
        return jnp.pad(w, ((0, 0), (0, 0), (0, ff_pad - ff_cols)))

    ff_part = jnp.concatenate(
        [quarters(gate_proj), quarters(up_proj), quarters(down_proj.T)], axis=2
    )
    ff_part = quad_exchange(ff_part)
    both_z = jnp.stack(mine_first(lax.axis_index("zh"), attn_part, swap(attn_part, "zh")))
    attn_part = both_z.reshape(4 * rows, piece)
    o_at = piece - HD
    attn_part, ff_part = lax.optimization_barrier(
        (gather_four(attn_part, "y", 0), ff_part.reshape(4 * rows, 3 * ff_pad))
    )
    attn_half = gather_four(attn_part, "x", 0).reshape(width, piece)
    kv_to = HD + half_cols
    qkv_half, gain_all = attn_half[:, :kv_to], attn_half[:, kv_to:o_at]
    qkv_two = mine_first(tee, qkv_half, swap(qkv_half, "t"))
    out_half = after(attn_half[:, o_at:], *qkv_two)
    out_two = mine_first(tee, out_half, swap(out_half, "t"))
    qkv_own = jnp.concatenate(
        [
            qkv_two[0][:, :HD],
            qkv_two[1][:, :HD],
            qkv_two[0][:, HD:],
            qkv_two[1][:, HD:],
        ],
        axis=1,
    )
    out_own = jnp.concatenate([out_two[0], out_two[1]], axis=1)
    qkv_all = jnp.concatenate([qkv_own, swap(qkv_own, "core")], axis=1)
    out_all = jnp.concatenate([out_own, swap(out_own, "core")], axis=1)
    pick = (
        lax.broadcasted_iota(jnp.int32, (8, LANES), 0)
        == lax.broadcasted_iota(jnp.int32, (8, LANES), 1)
    ).astype(bf16)
    gain_rows = matmul_nt(pick, gain_all)
    pre_gain, post_gain, ffn_gain, end_gain = (gain_rows[k] for k in range(4))

    def head_gain(k):
        part = gain_rows[k].reshape(4, 4, 2, 2, rows)[..., :head_rows]
        return part.transpose(0, 2, 1, 3, 4).reshape(HD)

    qgain, kgain = head_gain(4), head_gain(5)

    ff_all = lax.all_gather(
        ff_part, PLANE, axis=0, tiled=True
    )
    gate_all, up_all, down_all = (
        ff_all[:, k * ff_pad : (k + 1) * ff_pad] for k in range(3)
    )

    resid = matmul(inputs, turn)
    grad_out = matmul(cotangent, turn)
    segment = doc_ids[0]
    order = jnp.arange(seq_length, dtype=jnp.int32)
    own_seg = lax.dynamic_slice_in_dim(segment, tee * tokens, tokens)
    own_at = tee * tokens + jnp.arange(tokens, dtype=jnp.int32)
    peer_seg = lax.dynamic_slice_in_dim(segment, (1 - tee) * tokens, tokens)
    peer_at = (1 - tee) * tokens + jnp.arange(tokens, dtype=jnp.int32)
    position = jnp.sum(
        jnp.where(
            (own_seg[:, None] == segment[None, :]) & (order[None, :] < own_at[:, None]), 1, 0
        ).astype(jnp.int32),
        axis=1,
    ).astype(f32)
    rates = jnp.exp(jnp.arange(HD // 2, dtype=f32) * (-2.0 * math.log(rope_base) / HD))
    angles = position[:, None] * rates[None, :]
    cos_tab, sin_tab = jnp.cos(angles), jnp.sin(angles)
    key_seg = jnp.concatenate([own_seg, peer_seg])
    key_at = jnp.concatenate([own_at, peer_at])
    allowed = (own_seg[:, None] == key_seg[None, :]) & (key_at[None, :] <= own_at[:, None])
    mask_rows = jnp.tile(allowed, (H, 1))

    normed_f, in_back = jax.vjp(rms_scale, resid, pre_gain)
    normed_in = normed_f.astype(bf16)
    qkv = matmul(normed_in, qkv_all)
    n_qkv = 3 * HD
    q_raw = jnp.stack([qkv[:, a : a + HD] for a in (0, HD, n_qkv, n_qkv + HD)])
    k_raw, v_raw = mine_first(core, qkv[:, 2 * HD : n_qkv], qkv[:, n_qkv + 2 * HD :])
    q_full, q_back = jax.vjp(partial(head_piece, cos_tab, sin_tab, query_scale), q_raw, qgain)
    k_full, k_back = jax.vjp(partial(head_piece, cos_tab, sin_tab, 1.0), k_raw, kgain)
    query_rows = q_full.astype(bf16).reshape(H * tokens, HD)
    kv_own = jnp.concatenate([k_full.astype(bf16), v_raw.astype(bf16)], axis=1)
    kv_both = jnp.concatenate([kv_own, swap(kv_own, "t")], axis=0)
    keys_b, values_b = kv_both[:, :HD], kv_both[:, HD:]
    scores = matmul_nt(query_rows, keys_b)
    exp_scores = jnp.where(mask_rows, jnp.exp(scores), 0.0)
    log_total = jnp.log(jnp.sum(exp_scores, axis=1, keepdims=True))
    probs_f = jnp.where(mask_rows, jnp.exp(scores - log_total), 0.0)
    probs_b = probs_f.astype(bf16)
    mixed_rows = matmul(probs_b, values_b).astype(bf16)

    def side_by_side(head_rows_of):
        return jnp.concatenate(
            [head_rows_of[h * tokens : (h + 1) * tokens] for h in range(H)], axis=1
        )

    def stacked(cols):
        return jnp.concatenate([cols[:, h * HD : (h + 1) * HD] for h in range(H)], axis=0)

    mixed = side_by_side(mixed_rows)
    branch = matmul_nt(mixed, out_all)
    attn_norm, attn_back = jax.vjp(rms_scale, branch, post_gain)
    hidden = resid + attn_norm

    ff_norm, ff_in_back = jax.vjp(rms_scale, hidden, ffn_gain)

    def ff_forward(chunk):
        product, mix_back = jax.vjp(gelu_mix, matmul(chunk, gate_all), matmul(chunk, up_all))
        act = product.astype(bf16)
        return rows_first(matmul_nt(act, down_all)), act, mix_back

    ff_chunks = group_chunks(ff_norm.astype(bf16))
    done = [ff_forward(chunk) for chunk in ff_chunks]
    homes = [chunk_home(done[place][0], place) for place in range(4)]
    acts, mix_backs = [d[1] for d in done], [d[2] for d in done]
    ff_branch = homes[0] + (homes[1] + homes[2] + homes[3])
    end_norm, end_back = jax.vjp(rms_scale, ff_branch, end_gain)
    layer_out = matmul_nt((hidden + end_norm).astype(bf16), turn).astype(bf16)

    d_ff, grad_end = end_back(grad_out)

    def ff_backward(chunk, place):
        d_gate, d_up = mix_backs[place](matmul(chunk, down_all))
        d_gate, d_up = d_gate.astype(bf16), d_up.astype(bf16)
        d_chunk = matmul_nt(d_gate, gate_all) + matmul_nt(d_up, up_all)
        return rows_first(d_chunk), d_gate, d_up

    d_ff_chunks = group_chunks(d_ff.astype(bf16))
    done = [ff_backward(d_ff_chunks[place], place) for place in range(4)]
    homes = [chunk_home(done[place][0], place) for place in range(4)]
    ff_input, act, d_ff_rows, d_gate, d_up = (
        jnp.concatenate(lax.optimization_barrier(parts), axis=0)
        for parts in (
            ff_chunks,
            acts,
            d_ff_chunks,
            [d[1] for d in done],
            [d[2] for d in done],
        )
    )
    ff_input, act, d_ff_rows, d_gate, d_up, *_ = lax.optimization_barrier(
        (ff_input, act, d_ff_rows, d_gate, d_up, *(d[0] for d in done))
    )
    ff_grads = jnp.concatenate(
        [
            matmul_tn(ff_input, d_gate).astype(bf16),
            matmul_tn(ff_input, d_up).astype(bf16),
            matmul_tn(d_ff_rows, act).astype(bf16),
        ],
        axis=1,
    )
    d_ff_input = homes[0] + (homes[1] + homes[2] + homes[3])
    d_ff_input = after(d_ff_input, ff_grads)
    ff_sums = lax.psum_scatter(rows_first(ff_grads), PLANE, scatter_dimension=0, tiled=True)
    d_h_part, grad_ffn = ff_in_back(d_ff_input)
    d_hidden = grad_out + d_h_part

    d_branch, grad_post = attn_back(d_hidden)
    d_branch_b = d_branch.astype(bf16)
    out_grad = rows_first(matmul_tn(d_branch_b, mixed).astype(bf16))
    d_mixed = matmul(d_branch_b, out_all).astype(bf16)
    d_mixed_rows = stacked(d_mixed)
    delta = jnp.sum(
        d_mixed_rows.astype(f32) * mixed_rows.astype(f32), axis=1, keepdims=True
    )
    d_probs = matmul_nt(d_mixed_rows, values_b)
    d_scores = (probs_f * (d_probs - delta)).astype(bf16)
    d_queries = matmul(d_scores, keys_b).reshape(H, tokens, HD)
    d_kv = jnp.concatenate(
        [matmul_tn(d_scores, query_rows), matmul_tn(probs_b, d_mixed_rows)], axis=1
    )
    d_kv = d_kv[:tokens] + swap(d_kv[tokens:].astype(bf16), "t").astype(f32)
    d_keys, d_values = d_kv[:, :HD], d_kv[:, HD:]
    d_q_raw, grad_qgain = q_back(d_queries)
    d_k_raw, grad_kgain = k_back(d_keys)
    d_own, d_sib = mine_first(core, d_k_raw.astype(bf16), d_values.astype(bf16))
    d_q_b = d_q_raw.astype(bf16)
    d_qkv = jnp.concatenate([d_q_b[0], d_q_b[1], d_own, d_q_b[2], d_q_b[3], d_sib], axis=1)
    qkv_grad = rows_first(matmul_tn(normed_in, d_qkv).astype(bf16))
    d_normed = matmul_nt(d_qkv, qkv_all)
    d_in_part, grad_pre = in_back(d_normed)
    inputs_grad = jnp.dot(
        d_hidden + d_in_part,
        turn.T.astype(f32),
        precision=lax.Precision.HIGHEST,
        preferred_element_type=f32,
    )

    def turned_head(grad):
        grad = grad.reshape(4, 2, 4, 2, head_rows).transpose(0, 2, 1, 3, 4)
        return jnp.pad(grad, ((0, 0),) * 4 + ((0, rows - head_rows),)).reshape(width)

    gain_sets = [
        jnp.pad(jnp.stack(three), ((0, 5), (0, 0))).astype(bf16)
        for three in (
            (grad_pre, grad_post, grad_ffn),
            (grad_end, turned_head(grad_qgain), turned_head(grad_kgain)),
        )
    ]
    gain_own, gain_sib = (
        matmul_tn(g, pick).astype(bf16) for g in mine_first(core, gain_sets[0], gain_sets[1])
    )

    def core_sum(own, sib):
        return (own.astype(f32) + swap(sib, "core").astype(f32)).astype(bf16)

    qkv_sum = plane_sum(core_sum(qkv_grad[:, :n_qkv], qkv_grad[:, n_qkv:]), "y", "x")
    out_sum = plane_sum(
        core_sum(
            jnp.concatenate([out_grad[:, : 2 * HD], gain_own], axis=1),
            jnp.concatenate([out_grad[:, 2 * HD :], gain_sib], axis=1),
        ),
        "x",
        "y",
    )
    qkv_sum, out_sum, ff_sums, inputs_grad = lax.optimization_barrier(
        (qkv_sum, out_sum, ff_sums, inputs_grad)
    )
    ff_sums = quad_exchange(ff_sums.reshape(4, rows, 3 * ff_pad))

    def joined(k):
        part = ff_sums[:, :, k * ff_pad : k * ff_pad + ff_cols]
        return part.transpose(1, 0, 2).reshape(rows, 4 * ff_cols).astype(f32)

    sent_gate, sent_up, sent_down = joined(0), joined(1), joined(2).T
    shared = (qkv_sum[:, 2 * HD :], out_sum[:, 2 * HD :])
    for_tee = [
        jnp.concatenate(
            [part[:, k * HD : (k + 1) * HD] for part in (qkv_sum, out_sum)] + [*shared],
            axis=1,
        ).reshape(2, 1, 2 * rows, 3 * HD + LANES)
        for k in range(2)
    ]
    sums = jnp.concatenate(for_tee, axis=1).reshape(4, 2 * rows, 3 * HD + LANES)
    sums = ring_sum(sums).reshape(2, rows, 3 * HD + LANES)
    own, theirs = mine_first(core, sums[0], sums[1])
    sum_0, sum_1 = mine_first(core, own, swap(theirs, "core"))
    sent_query = jnp.concatenate([sum_0[:, :HD], sum_1[:, :HD]], axis=1)
    sent_outw = jnp.concatenate([sum_0[:, HD : 2 * HD], sum_1[:, HD : 2 * HD]], axis=1).T
    sent_key, sent_value = sum_0[:, 2 * HD : 3 * HD], sum_1[:, 2 * HD : 3 * HD]
    sent_pre, sent_post, sent_ffn = (sum_0[:, 3 * HD + k] for k in range(3))
    sent_end = sum_1[:, 3 * HD]
    sent_qgain, sent_kgain = (sum_1[:head_rows, 3 * HD + k] for k in (1, 2))
    return (
        layer_out,
        inputs_grad,
        sent_pre,
        sent_query,
        sent_key,
        sent_value,
        sent_qgain,
        sent_kgain,
        sent_outw,
        sent_post,
        sent_ffn,
        sent_gate,
        sent_up,
        sent_down,
        sent_end,
    )


def solution(mesh):
    parts = Mesh(mesh.devices.reshape(SIZES), AXES)
    every = (*DP, "t")
    return jax.shard_map(
        on_device,
        mesh=parts,
        in_specs=(
            P(every, None),
            P(DP, None),
            P(DP),
            P(DP, "t"),
            P(DP, None),
            P(DP, None),
            P(DP),
            P(DP),
            P("t", DP),
            P(DP),
            P(DP),
            P(DP, "t"),
            P(DP, "t"),
            P("t", DP),
            P(DP),
            P(every, None),
        ),
        out_specs=(
            P(every, None),
            P(every, None),
            P(DP),
            P(DP, "t"),
            P(DP, None),
            P(DP, None),
            P(DP),
            P(DP),
            P("t", DP),
            P(DP),
            P(DP),
            P(DP, "t"),
            P(DP, "t"),
            P("t", DP),
            P(DP),
        ),
        check_vma=False,
    )
```

```python
from functools import partial
import math

import jax
import jax.numpy as jnp
from jax import lax
from jax.experimental.layout import Layout, with_layout_constraint
from jax.sharding import Mesh, PartitionSpec as P

H = 4
HD = 256

epsilon = 1e-06
rope_base = 1000000.0
query_scale = 0.0625

AXES = ("x", "zh", "y", "core", "t")
SIZES = (4, 2, 4, 2, 2)
DP = ("x", "zh", "y", "core")
PLANE = ("x", "y")
ZRING = ("zh", "t")
QUAD = ("zh", "core")
LANES = 128

bf16 = jnp.bfloat16
f32 = jnp.float32


def rms_scale(values, scales):
    mean_sq = jnp.mean(values * values, axis=-1, keepdims=True)
    return values * lax.rsqrt(mean_sq + epsilon) * scales


def head_piece(cos_tab, sin_tab, factor, raw_heads, scales):
    normed = rms_scale(raw_heads, scales)
    half_width = normed.shape[-1] // 2
    first_half = normed[..., :half_width]
    second = normed[..., half_width:]
    turned = jnp.concatenate(
        [first_half * cos_tab - second * sin_tab, second * cos_tab + first_half * sin_tab],
        axis=-1,
    )
    return turned * factor


def gelu_mix(gate_in, up_in):
    return jax.nn.gelu(gate_in, approximate=True) * up_in


def matmul(left_op, right_op):
    return jnp.dot(left_op, right_op, preferred_element_type=f32)


def matmul_nt(left_op, right_op):
    return lax.dot_general(
        left_op, right_op, (((1,), (1,)), ((), ())), preferred_element_type=f32
    )


def rows_first(x):
    return with_layout_constraint(x, Layout(major_to_minor=(0, 1)))


def matmul_tn(left_op, right_op):
    return lax.dot_general(
        left_op, right_op, (((0,), (0,)), ((), ())), preferred_element_type=f32
    )


def along_z(x, step):
    return lax.ppermute(x, ZRING, [(i, (i + step) % 4) for i in range(4)])


def swap(x, axis):
    return lax.ppermute(x, axis, [(0, 1), (1, 0)])


def group_chunks(rows):
    far = along_z(rows, 2)
    near = (rows, along_z(rows, 1), along_z(rows, -1), far)
    return [jnp.concatenate([b, swap(b, "core")], axis=0) for b in near]


def chunk_home(part, place):
    n = part.shape[0] // 2
    both = part[:n] + swap(part[n:].astype(bf16), "core").astype(f32)
    step = (0, -1, 1, 2)[place]
    return along_z(both.astype(bf16), step).astype(f32) if step else both


def along(x, axis, step):
    return lax.ppermute(x, axis, [(i, (i + step) % 4) for i in range(4)])


def quad_exchange(x):
    me = lax.axis_index(QUAD)
    got = [lax.dynamic_index_in_dim(x, me, 0, keepdims=False)] + [
        lax.ppermute(
            lax.dynamic_index_in_dim(x, me ^ k, 0, keepdims=False),
            QUAD,
            [(i, i ^ k) for i in range(4)],
        )
        for k in (1, 2, 3)
    ]
    return jnp.stack([chosen(me ^ place, got) for place in range(4)])


def chosen(which, four):
    pair = [jnp.where(which % 2 == 0, four[k], four[k + 1]) for k in (0, 2)]
    return jnp.where(which < 2, pair[0], pair[1])


def ring_sum(x):
    me = lax.axis_index(ZRING)
    blocks = [lax.dynamic_index_in_dim(x, (me + k) % 4, 0, keepdims=False) for k in range(4)]
    back = [along_z(blocks[k], k).astype(f32) for k in (1, 2, 3)]
    return blocks[0].astype(f32) + (back[0] + back[1] + back[2])


def after(x, *others):
    return lax.optimization_barrier((x, *others))[0]


def gather_four(x, axis, dim):
    me = lax.axis_index(axis)
    out = jnp.zeros(x.shape[:dim] + (4,) + x.shape[dim:], x.dtype)
    for step in (1, -1, 2, 0):
        block = along(x, axis, step) if step else x
        out = lax.dynamic_update_index_in_dim(out, block, (me - step) % 4, dim)
    return out


def sum_four(x, axis):
    back = [along(x[k], axis, k) for k in (1, 2, 3)]
    return x[0].astype(f32) + (
        back[0].astype(f32) + back[1].astype(f32) + back[2].astype(f32)
    )


def plane_sum(x, first, second):
    x = x.reshape(4, 4, x.shape[0] // 16, x.shape[1])
    for axis in (first, second):
        dim = 1 if axis == "y" and axis == first else 0
        me = lax.axis_index(axis)
        blocks = [
            lax.dynamic_index_in_dim(x, (me + k) % 4, dim, keepdims=False) for k in range(4)
        ]
        x = sum_four([b.astype(bf16) for b in blocks], axis)
    return x.astype(bf16)


def mine_first(core, own, sib):
    return jnp.where(core == 0, own, sib), jnp.where(core == 0, sib, own)


def on_device(
    inputs,
    doc_ids,
    prenorm,
    query_proj,
    key_proj,
    value_proj,
    querynorm,
    keynorm,
    output_proj,
    postnorm,
    ffnnorm,
    gate_proj,
    up_proj,
    down_proj,
    endnorm,
    cotangent,
):
    core = lax.axis_index("core")
    tee = lax.axis_index("t")
    rows = prenorm.shape[0]
    head_rows = querynorm.shape[0]
    width = rows * 64
    tokens = inputs.shape[0]
    seq_length = doc_ids.shape[1]
    half_cols = HD // 2

    pos = lax.optimization_barrier(jnp.arange(width, dtype=jnp.int32))
    p_x, p_y, p_zh, p_in = (
        pos // (16 * rows),
        pos // (4 * rows) % 4,
        pos // (2 * rows) % 2,
        pos % (2 * rows),
    )
    natural = (p_x * 8 + p_zh * 4 + p_y) * (2 * rows) + p_in
    turn = (pos[:, None] == natural[None, :]).astype(bf16)

    kv_pair = (
        lax.dynamic_slice_in_dim(key_proj, tee * half_cols, half_cols, axis=1),
        lax.dynamic_slice_in_dim(value_proj, tee * half_cols, half_cols, axis=1),
    )
    out_t = output_proj.T
    gain_cols = jnp.stack(
        [
            prenorm,
            postnorm,
            ffnnorm,
            endnorm,
            jnp.pad(querynorm, (0, rows - head_rows)),
            jnp.pad(keynorm, (0, rows - head_rows)),
        ],
        axis=1,
    )
    gain_cols = jnp.pad(gain_cols, ((0, 0), (0, LANES - 6)))
    halves = [
        jnp.concatenate(
            [
                query_proj[:, c * HD : (c + 1) * HD],
                kv_pair[c],
                gain_cols,
                out_t[:, c * HD : (c + 1) * HD],
            ],
            axis=1,
        )
        for c in range(2)
    ]
    piece = halves[0].shape[1]
    keep, give = mine_first(core, halves[0], halves[1])
    got = swap(give, "core")
    first, second = mine_first(core, keep, got)
    attn_part = jnp.stack([first, second]).reshape(2 * rows, piece)
    both_z = jnp.stack(mine_first(lax.axis_index("zh"), attn_part, swap(attn_part, "zh")))
    attn_part = both_z.reshape(4 * rows, piece)
    attn_part, gate_proj, up_proj, down_proj = lax.optimization_barrier(
        (attn_part, gate_proj, up_proj, down_proj)
    )
    ff_cols = gate_proj.shape[1] // 4
    ff_pad = -(-ff_cols // LANES) * LANES

    def quarters(w):
        w = w.reshape(rows, 4, ff_cols).transpose(1, 0, 2)
        return jnp.pad(w, ((0, 0), (0, 0), (0, ff_pad - ff_cols)))

    ff_part = jnp.concatenate(
        [quarters(gate_proj), quarters(up_proj), quarters(down_proj.T)], axis=2
    )
    ff_part = quad_exchange(ff_part)
    o_at = piece - HD
    attn_part, ff_part = lax.optimization_barrier(
        (gather_four(attn_part, "y", 0), ff_part.reshape(4 * rows, 3 * ff_pad))
    )
    attn_half = gather_four(attn_part, "x", 0).reshape(width, piece)
    kv_to = HD + half_cols
    gain_all = attn_half[:, kv_to:o_at]

    own_w = attn_half[:, :kv_to]
    peer_w = swap(own_w, "t")
    qkv_w = (own_w, peer_w, swap(own_w, "core"), swap(peer_w, "core"))
    out_own = after(attn_half[:, o_at:], peer_w)
    out_peer = swap(out_own, "t")
    pick = (
        lax.broadcasted_iota(jnp.int32, (8, LANES), 0)
        == lax.broadcasted_iota(jnp.int32, (8, LANES), 1)
    ).astype(bf16)
    gain_rows = matmul_nt(pick, gain_all)
    pre_gain, post_gain, ffn_gain, end_gain = (gain_rows[k] for k in range(4))

    def head_gain(k):
        part = gain_rows[k].reshape(4, 4, 2, 2, rows)[..., :head_rows]
        return part.transpose(0, 2, 1, 3, 4).reshape(HD)

    qgain, kgain = head_gain(4), head_gain(5)

    ff_all = lax.all_gather(
        ff_part, PLANE, axis=0, tiled=True
    )
    gate_all, up_all, down_all = (
        ff_all[:, k * ff_pad : (k + 1) * ff_pad] for k in range(3)
    )

    resid = matmul(inputs, turn)
    grad_out = matmul(cotangent, turn)
    segment = doc_ids[0]
    order = jnp.arange(seq_length, dtype=jnp.int32)
    own_seg = lax.dynamic_slice_in_dim(segment, tee * tokens, tokens)
    own_at = tee * tokens + jnp.arange(tokens, dtype=jnp.int32)
    peer_seg = lax.dynamic_slice_in_dim(segment, (1 - tee) * tokens, tokens)
    peer_at = (1 - tee) * tokens + jnp.arange(tokens, dtype=jnp.int32)
    position = jnp.sum(
        jnp.where(
            (own_seg[:, None] == segment[None, :]) & (order[None, :] < own_at[:, None]), 1, 0
        ).astype(jnp.int32),
        axis=1,
    ).astype(f32)
    rates = jnp.exp(jnp.arange(HD // 2, dtype=f32) * (-2.0 * math.log(rope_base) / HD))
    angles = position[:, None] * rates[None, :]
    cos_tab, sin_tab = jnp.cos(angles), jnp.sin(angles)
    key_seg = jnp.concatenate([own_seg, peer_seg])
    key_at = jnp.concatenate([own_at, peer_at])
    allowed = (own_seg[:, None] == key_seg[None, :]) & (key_at[None, :] <= own_at[:, None])
    mask_rows = jnp.tile(allowed, (H, 1))

    normed_f, in_back = jax.vjp(rms_scale, resid, pre_gain)
    normed_in = normed_f.astype(bf16)
    n_qkv = 3 * HD
    qkv = [matmul(normed_in, w) for w in qkv_w]
    q_raw = jnp.stack([r[:, :HD] for r in qkv])
    kv = [
        jnp.concatenate(mine_first(tee, a[:, HD:], b[:, HD:]), axis=1)
        for a, b in (qkv[:2], qkv[2:])
    ]
    k_raw, v_raw = mine_first(core, kv[0], kv[1])
    q_full, q_back = jax.vjp(partial(head_piece, cos_tab, sin_tab, query_scale), q_raw, qgain)
    k_full, k_back = jax.vjp(partial(head_piece, cos_tab, sin_tab, 1.0), k_raw, kgain)
    query_rows = q_full.astype(bf16).reshape(H * tokens, HD)
    kv_own = jnp.concatenate([k_full.astype(bf16), v_raw.astype(bf16)], axis=1)
    kv_both = jnp.concatenate([kv_own, swap(kv_own, "t")], axis=0)
    out_peer = after(out_peer, kv_own)
    out_w = (out_own, out_peer, swap(out_own, "core"), swap(out_peer, "core"))
    keys_b, values_b = kv_both[:, :HD], kv_both[:, HD:]
    scores = matmul_nt(query_rows, keys_b)
    exp_scores = jnp.where(mask_rows, jnp.exp(scores), 0.0)
    log_total = jnp.log(jnp.sum(exp_scores, axis=1, keepdims=True))
    probs_f = jnp.where(mask_rows, jnp.exp(scores - log_total), 0.0)
    probs_b = probs_f.astype(bf16)
    mixed_rows = matmul(probs_b, values_b).astype(bf16)

    def head_of(x, h):
        return x[h * tokens : (h + 1) * tokens]

    def by_tee(four, dim):
        return jnp.concatenate(
            [*mine_first(tee, *four[:2]), *mine_first(tee, *four[2:])], axis=dim
        )

    branches = [matmul_nt(head_of(mixed_rows, h), out_w[h]) for h in range(H)]
    branch = (branches[0] + branches[1]) + (branches[2] + branches[3])
    mixed = by_tee([head_of(mixed_rows, h) for h in range(H)], 1)
    attn_norm, attn_back = jax.vjp(rms_scale, branch, post_gain)
    hidden = resid + attn_norm

    ff_norm, ff_in_back = jax.vjp(rms_scale, hidden, ffn_gain)

    def ff_forward(chunk):
        product, mix_back = jax.vjp(gelu_mix, matmul(chunk, gate_all), matmul(chunk, up_all))
        act = product.astype(bf16)
        return rows_first(matmul_nt(act, down_all)), act, mix_back

    ff_chunks = group_chunks(ff_norm.astype(bf16))
    done = [ff_forward(chunk) for chunk in ff_chunks]
    homes = [chunk_home(done[place][0], place) for place in range(4)]
    acts, mix_backs = [d[1] for d in done], [d[2] for d in done]
    ff_branch = homes[0] + (homes[1] + homes[2] + homes[3])
    end_norm, end_back = jax.vjp(rms_scale, ff_branch, end_gain)
    layer_out = matmul_nt((hidden + end_norm).astype(bf16), turn).astype(bf16)

    d_ff, grad_end = end_back(grad_out)

    def ff_backward(chunk, place):
        d_gate, d_up = mix_backs[place](matmul(chunk, down_all))
        d_gate, d_up = d_gate.astype(bf16), d_up.astype(bf16)
        d_chunk = matmul_nt(d_gate, gate_all) + matmul_nt(d_up, up_all)
        return rows_first(d_chunk), d_gate, d_up

    d_ff_chunks = group_chunks(d_ff.astype(bf16))
    done = [ff_backward(d_ff_chunks[place], place) for place in range(4)]
    homes = [chunk_home(done[place][0], place) for place in range(4)]
    ff_input, act, d_ff_rows, d_gate, d_up = (
        jnp.concatenate(lax.optimization_barrier(parts), axis=0)
        for parts in (
            ff_chunks,
            acts,
            d_ff_chunks,
            [d[1] for d in done],
            [d[2] for d in done],
        )
    )
    ff_input, act, d_ff_rows, d_gate, d_up, *_ = lax.optimization_barrier(
        (ff_input, act, d_ff_rows, d_gate, d_up, *(d[0] for d in done))
    )
    ff_grads = jnp.concatenate(
        [
            matmul_tn(ff_input, d_gate).astype(bf16),
            matmul_tn(ff_input, d_up).astype(bf16),
            matmul_tn(d_ff_rows, act).astype(bf16),
        ],
        axis=1,
    )
    d_ff_input = homes[0] + (homes[1] + homes[2] + homes[3])
    d_ff_input = after(d_ff_input, ff_grads)
    ff_sums = lax.psum_scatter(rows_first(ff_grads), PLANE, scatter_dimension=0, tiled=True)
    d_h_part, grad_ffn = ff_in_back(d_ff_input)
    d_hidden = grad_out + d_h_part

    d_branch, grad_post = attn_back(d_hidden)
    d_branch_b = d_branch.astype(bf16)
    out_grad = rows_first(matmul_tn(d_branch_b, mixed).astype(bf16))
    d_mixed_rows = jnp.concatenate([matmul(d_branch_b, w).astype(bf16) for w in out_w], axis=0)
    delta = jnp.sum(
        d_mixed_rows.astype(f32) * mixed_rows.astype(f32), axis=1, keepdims=True
    )
    d_probs = matmul_nt(d_mixed_rows, values_b)
    d_scores = (probs_f * (d_probs - delta)).astype(bf16)
    d_queries = matmul(d_scores, keys_b).reshape(H, tokens, HD)
    d_kv = jnp.concatenate(
        [matmul_tn(d_scores, query_rows), matmul_tn(probs_b, d_mixed_rows)], axis=1
    )
    d_kv = d_kv[:tokens] + swap(d_kv[tokens:].astype(bf16), "t").astype(f32)
    d_keys, d_values = d_kv[:, :HD], d_kv[:, HD:]
    d_q_raw, grad_qgain = q_back(d_queries)
    d_k_raw, grad_kgain = k_back(d_keys)
    d_own, d_sib = mine_first(core, d_k_raw.astype(bf16), d_values.astype(bf16))
    d_q_b = d_q_raw.astype(bf16)
    d_side = [
        part
        for d in (d_own, d_sib)
        for part in mine_first(tee, d[:, :half_cols], d[:, half_cols:])
    ]
    d_normeds = [
        matmul_nt(jnp.concatenate([d_q_b[h], d_side[h]], axis=1), qkv_w[h]) for h in range(H)
    ]
    d_normed = (d_normeds[0] + d_normeds[1]) + (d_normeds[2] + d_normeds[3])
    d_q_two = by_tee([d_q_b[h] for h in range(H)], 1)
    d_qkv = jnp.concatenate(
        [d_q_two[:, : 2 * HD], d_own, d_q_two[:, 2 * HD :], d_sib], axis=1
    )
    qkv_grad = rows_first(matmul_tn(normed_in, d_qkv).astype(bf16))
    d_in_part, grad_pre = in_back(d_normed)
    inputs_grad = jnp.dot(
        d_hidden + d_in_part,
        turn.T.astype(f32),
        precision=lax.Precision.HIGHEST,
        preferred_element_type=f32,
    )

    def turned_head(grad):
        grad = grad.reshape(4, 2, 4, 2, head_rows).transpose(0, 2, 1, 3, 4)
        return jnp.pad(grad, ((0, 0),) * 4 + ((0, rows - head_rows),)).reshape(width)

    gain_sets = [
        jnp.pad(jnp.stack(three), ((0, 5), (0, 0))).astype(bf16)
        for three in (
            (grad_pre, grad_post, grad_ffn),
            (grad_end, turned_head(grad_qgain), turned_head(grad_kgain)),
        )
    ]
    gain_own, gain_sib = (
        matmul_tn(g, pick).astype(bf16) for g in mine_first(core, gain_sets[0], gain_sets[1])
    )

    def core_sum(own, sib):
        return (own.astype(f32) + swap(sib, "core").astype(f32)).astype(bf16)

    qkv_sum = plane_sum(core_sum(qkv_grad[:, :n_qkv], qkv_grad[:, n_qkv:]), "y", "x")
    out_sum = plane_sum(
        core_sum(
            jnp.concatenate([out_grad[:, : 2 * HD], gain_own], axis=1),
            jnp.concatenate([out_grad[:, 2 * HD :], gain_sib], axis=1),
        ),
        "x",
        "y",
    )
    qkv_sum, out_sum, ff_sums, inputs_grad = lax.optimization_barrier(
        (qkv_sum, out_sum, ff_sums, inputs_grad)
    )
    ff_sums = quad_exchange(ff_sums.reshape(4, rows, 3 * ff_pad))

    def joined(k):
        part = ff_sums[:, :, k * ff_pad : k * ff_pad + ff_cols]
        return part.transpose(1, 0, 2).reshape(rows, 4 * ff_cols).astype(f32)

    sent_gate, sent_up, sent_down = joined(0), joined(1), joined(2).T
    shared = (qkv_sum[:, 2 * HD :], out_sum[:, 2 * HD :])
    for_tee = [
        jnp.concatenate(
            [part[:, k * HD : (k + 1) * HD] for part in (qkv_sum, out_sum)] + [*shared],
            axis=1,
        ).reshape(2, 1, 2 * rows, 3 * HD + LANES)
        for k in range(2)
    ]
    sums = jnp.concatenate(for_tee, axis=1).reshape(4, 2 * rows, 3 * HD + LANES)
    sums = ring_sum(sums).reshape(2, rows, 3 * HD + LANES)
    own, theirs = mine_first(core, sums[0], sums[1])
    sum_0, sum_1 = mine_first(core, own, swap(theirs, "core"))
    sent_query = jnp.concatenate([sum_0[:, :HD], sum_1[:, :HD]], axis=1)
    sent_outw = jnp.concatenate([sum_0[:, HD : 2 * HD], sum_1[:, HD : 2 * HD]], axis=1).T
    sent_key, sent_value = sum_0[:, 2 * HD : 3 * HD], sum_1[:, 2 * HD : 3 * HD]
    sent_pre, sent_post, sent_ffn = (sum_0[:, 3 * HD + k] for k in range(3))
    sent_end = sum_1[:, 3 * HD]
    sent_qgain, sent_kgain = (sum_1[:head_rows, 3 * HD + k] for k in (1, 2))
    return (
        layer_out,
        inputs_grad,
        sent_pre,
        sent_query,
        sent_key,
        sent_value,
        sent_qgain,
        sent_kgain,
        sent_outw,
        sent_post,
        sent_ffn,
        sent_gate,
        sent_up,
        sent_down,
        sent_end,
    )


def solution(mesh):
    parts = Mesh(mesh.devices.reshape(SIZES), AXES)
    every = (*DP, "t")
    return jax.shard_map(
        on_device,
        mesh=parts,
        in_specs=(
            P(every, None),
            P(DP, None),
            P(DP),
            P(DP, "t"),
            P(DP, None),
            P(DP, None),
            P(DP),
            P(DP),
            P("t", DP),
            P(DP),
            P(DP),
            P(DP, "t"),
            P(DP, "t"),
            P("t", DP),
            P(DP),
            P(every, None),
        ),
        out_specs=(
            P(every, None),
            P(every, None),
            P(DP),
            P(DP, "t"),
            P(DP, None),
            P(DP, None),
            P(DP),
            P(DP),
            P("t", DP),
            P(DP),
            P(DP),
            P(DP, "t"),
            P(DP, "t"),
            P("t", DP),
            P(DP),
        ),
        check_vma=False,
    )
```

```python
from functools import partial
import math

import jax
import jax.numpy as jnp
from jax import lax
from jax.experimental.layout import Layout, with_layout_constraint
from jax.sharding import Mesh, PartitionSpec as P

H = 4
HD = 256

epsilon = 1e-06
rope_base = 1000000.0
query_scale = 0.0625

AXES = ("x", "zh", "y", "core", "t")
SIZES = (4, 2, 4, 2, 2)
DP = ("x", "zh", "y", "core")
PLANE = ("x", "y")
ZRING = ("zh", "t")
QUAD = ("zh", "core")
LANES = 128

bf16 = jnp.bfloat16
f32 = jnp.float32


def rms_scale(values, scales):
    mean_sq = jnp.mean(values * values, axis=-1, keepdims=True)
    return values * lax.rsqrt(mean_sq + epsilon) * scales


def head_piece(cos_tab, sin_tab, factor, raw_heads, scales):
    normed = rms_scale(raw_heads, scales)
    half_width = normed.shape[-1] // 2
    first_half = normed[..., :half_width]
    second = normed[..., half_width:]
    turned = jnp.concatenate(
        [first_half * cos_tab - second * sin_tab, second * cos_tab + first_half * sin_tab],
        axis=-1,
    )
    return turned * factor


def gelu_mix(gate_in, up_in):
    return jax.nn.gelu(gate_in, approximate=True) * up_in


def matmul(left_op, right_op):
    return jnp.dot(left_op, right_op, preferred_element_type=f32)


def matmul_nt(left_op, right_op):
    return lax.dot_general(
        left_op, right_op, (((1,), (1,)), ((), ())), preferred_element_type=f32
    )


def rows_first(x):
    return with_layout_constraint(x, Layout(major_to_minor=(0, 1)))


def matmul_tn(left_op, right_op):
    return lax.dot_general(
        left_op, right_op, (((0,), (0,)), ((), ())), preferred_element_type=f32
    )


def along_z(x, step):
    return lax.ppermute(x, ZRING, [(i, (i + step) % 4) for i in range(4)])


def swap(x, axis):
    return lax.ppermute(x, axis, [(0, 1), (1, 0)])


def group_chunks(rows):
    far = along_z(rows, 2)
    near = (rows, along_z(rows, 1), along_z(rows, -1), far)
    return [jnp.concatenate([b, swap(b, "core")], axis=0) for b in near]


def chunk_home(part, place):
    n = part.shape[0] // 2
    both = part[:n] + swap(part[n:].astype(bf16), "core").astype(f32)
    step = (0, -1, 1, 2)[place]
    return along_z(both.astype(bf16), step).astype(f32) if step else both


def along(x, axis, step):
    return lax.ppermute(x, axis, [(i, (i + step) % 4) for i in range(4)])


def quad_exchange(x):
    me = lax.axis_index(QUAD)
    got = [lax.dynamic_index_in_dim(x, me, 0, keepdims=False)] + [
        lax.ppermute(
            lax.dynamic_index_in_dim(x, me ^ k, 0, keepdims=False),
            QUAD,
            [(i, i ^ k) for i in range(4)],
        )
        for k in (1, 2, 3)
    ]
    return jnp.stack([chosen(me ^ place, got) for place in range(4)])


def chosen(which, four):
    pair = [jnp.where(which % 2 == 0, four[k], four[k + 1]) for k in (0, 2)]
    return jnp.where(which < 2, pair[0], pair[1])


def ring_sum(x):
    me = lax.axis_index(ZRING)
    blocks = [lax.dynamic_index_in_dim(x, (me + k) % 4, 0, keepdims=False) for k in range(4)]
    back = [along_z(blocks[k], k).astype(f32) for k in (1, 2, 3)]
    return blocks[0].astype(f32) + (back[0] + back[1] + back[2])


def after(x, *others):
    return lax.optimization_barrier((x, *others))[0]


def gather_four(x, axis, dim):
    me = lax.axis_index(axis)
    out = jnp.zeros(x.shape[:dim] + (4,) + x.shape[dim:], x.dtype)
    for step in (1, -1, 2, 0):
        block = along(x, axis, step) if step else x
        out = lax.dynamic_update_index_in_dim(out, block, (me - step) % 4, dim)
    return out


def sum_four(x, axis):
    back = [along(x[k], axis, k) for k in (1, 2, 3)]
    return x[0].astype(f32) + (
        back[0].astype(f32) + back[1].astype(f32) + back[2].astype(f32)
    )


def plane_sum(x, first, second):
    x = x.reshape(4, 4, x.shape[0] // 16, x.shape[1])
    for axis in (first, second):
        dim = 1 if axis == "y" and axis == first else 0
        me = lax.axis_index(axis)
        blocks = [
            lax.dynamic_index_in_dim(x, (me + k) % 4, dim, keepdims=False) for k in range(4)
        ]
        x = sum_four([b.astype(bf16) for b in blocks], axis)
    return x.astype(bf16)


def mine_first(core, own, sib):
    return jnp.where(core == 0, own, sib), jnp.where(core == 0, sib, own)


def on_device(
    inputs,
    doc_ids,
    prenorm,
    query_proj,
    key_proj,
    value_proj,
    querynorm,
    keynorm,
    output_proj,
    postnorm,
    ffnnorm,
    gate_proj,
    up_proj,
    down_proj,
    endnorm,
    cotangent,
):
    core = lax.axis_index("core")
    tee = lax.axis_index("t")
    rows = prenorm.shape[0]
    head_rows = querynorm.shape[0]
    width = rows * 64
    tokens = inputs.shape[0]
    seq_length = doc_ids.shape[1]
    half_cols = HD // 2

    pos = lax.optimization_barrier(jnp.arange(width, dtype=jnp.int32))
    p_x, p_y, p_zh, p_in = (
        pos // (16 * rows),
        pos // (4 * rows) % 4,
        pos // (2 * rows) % 2,
        pos % (2 * rows),
    )
    natural = (p_x * 8 + p_zh * 4 + p_y) * (2 * rows) + p_in
    turn = (pos[:, None] == natural[None, :]).astype(bf16)

    kv_pair = (
        lax.dynamic_slice_in_dim(key_proj, tee * half_cols, half_cols, axis=1),
        lax.dynamic_slice_in_dim(value_proj, tee * half_cols, half_cols, axis=1),
    )
    out_t = output_proj.T
    gain_cols = jnp.stack(
        [
            prenorm,
            postnorm,
            ffnnorm,
            endnorm,
            jnp.pad(querynorm, (0, rows - head_rows)),
            jnp.pad(keynorm, (0, rows - head_rows)),
        ],
        axis=1,
    )
    gain_cols = jnp.pad(gain_cols, ((0, 0), (0, LANES - 6)))
    halves = [
        jnp.concatenate(
            [
                query_proj[:, c * HD : (c + 1) * HD],
                kv_pair[c],
                gain_cols,
                out_t[:, c * HD : (c + 1) * HD],
            ],
            axis=1,
        )
        for c in range(2)
    ]
    piece = halves[0].shape[1]
    keep, give = mine_first(core, halves[0], halves[1])
    got = swap(give, "core")
    first, second = mine_first(core, keep, got)
    attn_part = jnp.stack([first, second]).reshape(2 * rows, piece)
    both_z = jnp.stack(mine_first(lax.axis_index("zh"), attn_part, swap(attn_part, "zh")))
    attn_part = both_z.reshape(4 * rows, piece)
    attn_part, gate_proj, up_proj, down_proj = lax.optimization_barrier(
        (attn_part, gate_proj, up_proj, down_proj)
    )
    ff_cols = gate_proj.shape[1] // 4
    ff_pad = -(-ff_cols // LANES) * LANES

    def quarters(w):
        w = w.reshape(rows, 4, ff_cols).transpose(1, 0, 2)
        return jnp.pad(w, ((0, 0), (0, 0), (0, ff_pad - ff_cols)))

    ff_part = jnp.concatenate(
        [quarters(gate_proj), quarters(up_proj), quarters(down_proj.T)], axis=2
    )
    ff_part = quad_exchange(ff_part)
    o_at = piece - HD
    attn_part, ff_part = lax.optimization_barrier(
        (gather_four(attn_part, "y", 0), ff_part.reshape(4 * rows, 3 * ff_pad))
    )
    attn_half = gather_four(attn_part, "x", 0).reshape(width, piece)
    kv_to = HD + half_cols
    gain_all = attn_half[:, kv_to:o_at]

    own_w = attn_half[:, :kv_to]
    peer_w = swap(own_w, "t")
    qkv_w = (own_w, peer_w, swap(own_w, "core"), swap(peer_w, "core"))
    out_own = after(attn_half[:, o_at:], peer_w)
    out_peer = swap(out_own, "t")
    pick = (
        lax.broadcasted_iota(jnp.int32, (8, LANES), 0)
        == lax.broadcasted_iota(jnp.int32, (8, LANES), 1)
    ).astype(bf16)
    gain_rows = matmul_nt(pick, gain_all)
    pre_gain, post_gain, ffn_gain, end_gain = (gain_rows[k] for k in range(4))

    def head_gain(k):
        part = gain_rows[k].reshape(4, 4, 2, 2, rows)[..., :head_rows]
        return part.transpose(0, 2, 1, 3, 4).reshape(HD)

    qgain, kgain = head_gain(4), head_gain(5)

    ff_all = lax.all_gather(
        ff_part, PLANE, axis=0, tiled=True
    )
    gate_all, up_all, down_all = (
        ff_all[:, k * ff_pad : (k + 1) * ff_pad] for k in range(3)
    )

    resid = matmul(inputs, turn)
    grad_out = matmul(cotangent, turn)
    segment = doc_ids[0]
    order = jnp.arange(seq_length, dtype=jnp.int32)
    own_seg = lax.dynamic_slice_in_dim(segment, tee * tokens, tokens)
    own_at = tee * tokens + jnp.arange(tokens, dtype=jnp.int32)
    peer_seg = lax.dynamic_slice_in_dim(segment, (1 - tee) * tokens, tokens)
    peer_at = (1 - tee) * tokens + jnp.arange(tokens, dtype=jnp.int32)
    position = jnp.sum(
        jnp.where(
            (own_seg[:, None] == segment[None, :]) & (order[None, :] < own_at[:, None]), 1, 0
        ).astype(jnp.int32),
        axis=1,
    ).astype(f32)
    rates = jnp.exp(jnp.arange(HD // 2, dtype=f32) * (-2.0 * math.log(rope_base) / HD))
    angles = position[:, None] * rates[None, :]
    cos_tab, sin_tab = jnp.cos(angles), jnp.sin(angles)
    key_seg = jnp.concatenate([own_seg, peer_seg])
    key_at = jnp.concatenate([own_at, peer_at])
    allowed = (own_seg[:, None] == key_seg[None, :]) & (key_at[None, :] <= own_at[:, None])
    mask_rows = jnp.tile(allowed, (H, 1))

    normed_f, in_back = jax.vjp(rms_scale, resid, pre_gain)
    normed_in = normed_f.astype(bf16)
    n_qkv = 3 * HD
    qkv = [matmul(normed_in, w) for w in qkv_w]
    q_raw = jnp.stack([r[:, :HD] for r in qkv])
    kv = [
        jnp.concatenate(mine_first(tee, a[:, HD:], b[:, HD:]), axis=1)
        for a, b in (qkv[:2], qkv[2:])
    ]
    k_raw, v_raw = mine_first(core, kv[0], kv[1])
    q_full, q_back = jax.vjp(partial(head_piece, cos_tab, sin_tab, query_scale), q_raw, qgain)
    k_full, k_back = jax.vjp(partial(head_piece, cos_tab, sin_tab, 1.0), k_raw, kgain)
    query_rows = q_full.astype(bf16).reshape(H * tokens, HD)
    kv_own = jnp.concatenate([k_full.astype(bf16), v_raw.astype(bf16)], axis=1)
    kv_both = jnp.concatenate([kv_own, swap(kv_own, "t")], axis=0)
    out_peer = after(out_peer, kv_own)
    out_w = (out_own, out_peer, swap(out_own, "core"), swap(out_peer, "core"))
    keys_b, values_b = kv_both[:, :HD], kv_both[:, HD:]
    scores = matmul_nt(query_rows, keys_b)
    exp_scores = jnp.where(mask_rows, jnp.exp(scores), 0.0)
    log_total = jnp.log(jnp.sum(exp_scores, axis=1, keepdims=True))
    probs_f = jnp.where(mask_rows, jnp.exp(scores - log_total), 0.0)
    probs_b = probs_f.astype(bf16)
    mixed_rows = matmul(probs_b, values_b).astype(bf16)

    def head_of(x, h):
        return x[h * tokens : (h + 1) * tokens]

    def by_tee(four, dim):
        return jnp.concatenate(
            [*mine_first(tee, *four[:2]), *mine_first(tee, *four[2:])], axis=dim
        )

    branches = [matmul_nt(head_of(mixed_rows, h), out_w[h]) for h in range(H)]
    branch = (branches[0] + branches[1]) + (branches[2] + branches[3])
    mixed = by_tee([head_of(mixed_rows, h) for h in range(H)], 1)
    attn_norm, attn_back = jax.vjp(rms_scale, branch, post_gain)
    hidden = resid + attn_norm

    ff_norm, ff_in_back = jax.vjp(rms_scale, hidden, ffn_gain)

    def ff_forward(chunk):
        product, mix_back = jax.vjp(gelu_mix, matmul(chunk, gate_all), matmul(chunk, up_all))
        act = product.astype(bf16)
        return rows_first(matmul_nt(act, down_all)), act, mix_back

    ff_chunks = group_chunks(ff_norm.astype(bf16))
    done = [ff_forward(chunk) for chunk in ff_chunks]
    homes = [chunk_home(done[place][0], place) for place in range(4)]
    acts, mix_backs = [d[1] for d in done], [d[2] for d in done]
    ff_branch = homes[0] + (homes[1] + homes[2] + homes[3])
    end_norm, end_back = jax.vjp(rms_scale, ff_branch, end_gain)
    layer_out = matmul_nt((hidden + end_norm).astype(bf16), turn).astype(bf16)

    d_ff, grad_end = end_back(grad_out)

    def ff_backward(chunk, place):
        d_gate, d_up = mix_backs[place](matmul(chunk, down_all))
        d_gate, d_up = d_gate.astype(bf16), d_up.astype(bf16)
        d_chunk = matmul_nt(d_gate, gate_all) + matmul_nt(d_up, up_all)
        return rows_first(d_chunk), d_gate, d_up

    d_ff_chunks = group_chunks(d_ff.astype(bf16))
    done = [ff_backward(d_ff_chunks[place], place) for place in range(4)]
    homes = [chunk_home(done[place][0], place) for place in range(4)]
    ff_input, act, d_ff_rows, d_gate, d_up = (
        jnp.concatenate(lax.optimization_barrier(parts), axis=0)
        for parts in (
            ff_chunks,
            acts,
            d_ff_chunks,
            [d[1] for d in done],
            [d[2] for d in done],
        )
    )
    ff_input, act, d_ff_rows, d_gate, d_up, *_ = lax.optimization_barrier(
        (ff_input, act, d_ff_rows, d_gate, d_up, *(d[0] for d in done))
    )
    ff_grads = jnp.concatenate(
        [
            matmul_tn(ff_input, d_gate).astype(bf16),
            matmul_tn(ff_input, d_up).astype(bf16),
            matmul_tn(d_ff_rows, act).astype(bf16),
        ],
        axis=1,
    )
    d_ff_input = homes[0] + (homes[1] + homes[2] + homes[3])
    d_ff_input = after(d_ff_input, ff_grads)
    ff_sums = lax.psum_scatter(rows_first(ff_grads), PLANE, scatter_dimension=0, tiled=True)
    d_h_part, grad_ffn = ff_in_back(d_ff_input)
    d_hidden = grad_out + d_h_part

    d_branch, grad_post = attn_back(d_hidden)
    d_branch_b = d_branch.astype(bf16)
    out_grad = rows_first(matmul_tn(d_branch_b, mixed).astype(bf16))
    d_mixed_rows = jnp.concatenate([matmul(d_branch_b, w).astype(bf16) for w in out_w], axis=0)
    delta = jnp.sum(
        d_mixed_rows.astype(f32) * mixed_rows.astype(f32), axis=1, keepdims=True
    )
    d_probs = matmul_nt(d_mixed_rows, values_b)
    d_scores = (probs_f * (d_probs - delta)).astype(bf16)
    d_queries = matmul(d_scores, keys_b).reshape(H, tokens, HD)
    d_kv = jnp.concatenate(
        [matmul_tn(d_scores, query_rows), matmul_tn(probs_b, d_mixed_rows)], axis=1
    )
    d_kv = d_kv[:tokens] + swap(d_kv[tokens:].astype(bf16), "t").astype(f32)
    d_keys, d_values = d_kv[:, :HD], d_kv[:, HD:]
    d_q_raw, grad_qgain = q_back(d_queries)
    d_k_raw, grad_kgain = k_back(d_keys)
    d_own, d_sib = mine_first(core, d_k_raw.astype(bf16), d_values.astype(bf16))
    d_q_b = d_q_raw.astype(bf16)
    d_side = [
        part
        for d in (d_own, d_sib)
        for part in mine_first(tee, d[:, :half_cols], d[:, half_cols:])
    ]
    d_q_two = by_tee([d_q_b[h] for h in range(H)], 1)
    d_qkv = jnp.concatenate(
        [d_q_two[:, : 2 * HD], d_own, d_q_two[:, 2 * HD :], d_sib], axis=1
    )
    qkv_grad = rows_first(matmul_tn(normed_in, d_qkv).astype(bf16))
    def core_sum(own, sib):
        return (own.astype(f32) + swap(sib, "core").astype(f32)).astype(bf16)

    qkv_cores = core_sum(qkv_grad[:, :n_qkv], qkv_grad[:, n_qkv:])
    qkv_cores, *late = lax.optimization_barrier((qkv_cores, *d_side, *(d_q_b[h] for h in range(H))))
    d_normeds = [
        matmul_nt(jnp.concatenate([late[H + h], late[h]], axis=1), qkv_w[h]) for h in range(H)
    ]
    d_normed = (d_normeds[0] + d_normeds[1]) + (d_normeds[2] + d_normeds[3])
    d_in_part, grad_pre = in_back(d_normed)
    inputs_grad = jnp.dot(
        d_hidden + d_in_part,
        turn.T.astype(f32),
        precision=lax.Precision.HIGHEST,
        preferred_element_type=f32,
    )

    def turned_head(grad):
        grad = grad.reshape(4, 2, 4, 2, head_rows).transpose(0, 2, 1, 3, 4)
        return jnp.pad(grad, ((0, 0),) * 4 + ((0, rows - head_rows),)).reshape(width)

    gain_sets = [
        jnp.pad(jnp.stack(three), ((0, 5), (0, 0))).astype(bf16)
        for three in (
            (grad_pre, grad_post, grad_ffn),
            (grad_end, turned_head(grad_qgain), turned_head(grad_kgain)),
        )
    ]
    gain_own, gain_sib = (
        matmul_tn(g, pick).astype(bf16) for g in mine_first(core, gain_sets[0], gain_sets[1])
    )

    qkv_sum = plane_sum(qkv_cores, "y", "x")
    out_sum = plane_sum(
        core_sum(
            jnp.concatenate([out_grad[:, : 2 * HD], gain_own], axis=1),
            jnp.concatenate([out_grad[:, 2 * HD :], gain_sib], axis=1),
        ),
        "x",
        "y",
    )
    qkv_sum, out_sum, ff_sums, inputs_grad = lax.optimization_barrier(
        (qkv_sum, out_sum, ff_sums, inputs_grad)
    )
    ff_sums = quad_exchange(ff_sums.reshape(4, rows, 3 * ff_pad))

    def joined(k):
        part = ff_sums[:, :, k * ff_pad : k * ff_pad + ff_cols]
        return part.transpose(1, 0, 2).reshape(rows, 4 * ff_cols).astype(f32)

    sent_gate, sent_up, sent_down = joined(0), joined(1), joined(2).T
    shared = (qkv_sum[:, 2 * HD :], out_sum[:, 2 * HD :])
    for_tee = [
        jnp.concatenate(
            [part[:, k * HD : (k + 1) * HD] for part in (qkv_sum, out_sum)] + [*shared],
            axis=1,
        ).reshape(2, 1, 2 * rows, 3 * HD + LANES)
        for k in range(2)
    ]
    sums = jnp.concatenate(for_tee, axis=1).reshape(4, 2 * rows, 3 * HD + LANES)
    sums = ring_sum(sums).reshape(2, rows, 3 * HD + LANES)
    own, theirs = mine_first(core, sums[0], sums[1])
    sum_0, sum_1 = mine_first(core, own, swap(theirs, "core"))
    sent_query = jnp.concatenate([sum_0[:, :HD], sum_1[:, :HD]], axis=1)
    sent_outw = jnp.concatenate([sum_0[:, HD : 2 * HD], sum_1[:, HD : 2 * HD]], axis=1).T
    sent_key, sent_value = sum_0[:, 2 * HD : 3 * HD], sum_1[:, 2 * HD : 3 * HD]
    sent_pre, sent_post, sent_ffn = (sum_0[:, 3 * HD + k] for k in range(3))
    sent_end = sum_1[:, 3 * HD]
    sent_qgain, sent_kgain = (sum_1[:head_rows, 3 * HD + k] for k in (1, 2))
    return (
        layer_out,
        inputs_grad,
        sent_pre,
        sent_query,
        sent_key,
        sent_value,
        sent_qgain,
        sent_kgain,
        sent_outw,
        sent_post,
        sent_ffn,
        sent_gate,
        sent_up,
        sent_down,
        sent_end,
    )


def solution(mesh):
    parts = Mesh(mesh.devices.reshape(SIZES), AXES)
    every = (*DP, "t")
    return jax.shard_map(
        on_device,
        mesh=parts,
        in_specs=(
            P(every, None),
            P(DP, None),
            P(DP),
            P(DP, "t"),
            P(DP, None),
            P(DP, None),
            P(DP),
            P(DP),
            P("t", DP),
            P(DP),
            P(DP),
            P(DP, "t"),
            P(DP, "t"),
            P("t", DP),
            P(DP),
            P(every, None),
        ),
        out_specs=(
            P(every, None),
            P(every, None),
            P(DP),
            P(DP, "t"),
            P(DP, None),
            P(DP, None),
            P(DP),
            P(DP),
            P("t", DP),
            P(DP),
            P(DP),
            P(DP, "t"),
            P(DP, "t"),
            P("t", DP),
            P(DP),
        ),
        check_vma=False,
    )
```

```python
from functools import partial
import math

import jax
import jax.numpy as jnp
from jax import lax
from jax.experimental.layout import Layout, with_layout_constraint
from jax.sharding import Mesh, PartitionSpec as P

H = 4
HD = 256

epsilon = 1e-06
rope_base = 1000000.0
query_scale = 0.0625

AXES = ("x", "zh", "y", "core", "t")
SIZES = (4, 2, 4, 2, 2)
DP = ("x", "zh", "y", "core")
PLANE = ("x", "y")
ZRING = ("zh", "t")
QUAD = ("zh", "core")
LANES = 128

bf16 = jnp.bfloat16
f32 = jnp.float32


def rms_scale(values, scales):
    mean_sq = jnp.mean(values * values, axis=-1, keepdims=True)
    return values * lax.rsqrt(mean_sq + epsilon) * scales


def head_piece(cos_tab, sin_tab, factor, raw_heads, scales):
    normed = rms_scale(raw_heads, scales)
    half_width = normed.shape[-1] // 2
    first_half = normed[..., :half_width]
    second = normed[..., half_width:]
    turned = jnp.concatenate(
        [first_half * cos_tab - second * sin_tab, second * cos_tab + first_half * sin_tab],
        axis=-1,
    )
    return turned * factor


def gelu_mix(gate_in, up_in):
    return jax.nn.gelu(gate_in, approximate=True) * up_in


def matmul(left_op, right_op):
    return jnp.dot(left_op, right_op, preferred_element_type=f32)


def matmul_nt(left_op, right_op):
    return lax.dot_general(
        left_op, right_op, (((1,), (1,)), ((), ())), preferred_element_type=f32
    )


def rows_first(x):
    return with_layout_constraint(x, Layout(major_to_minor=(0, 1)))


def matmul_tn(left_op, right_op):
    return lax.dot_general(
        left_op, right_op, (((0,), (0,)), ((), ())), preferred_element_type=f32
    )


def along_z(x, step):
    return lax.ppermute(x, ZRING, [(i, (i + step) % 4) for i in range(4)])


def swap(x, axis):
    return lax.ppermute(x, axis, [(0, 1), (1, 0)])


def group_chunks(rows):
    far = along_z(rows, 2)
    near = (rows, along_z(rows, 1), along_z(rows, -1), far)
    return [jnp.concatenate([b, swap(b, "core")], axis=0) for b in near]


def chunk_home(part, place):
    n = part.shape[0] // 2
    both = part[:n] + swap(part[n:].astype(bf16), "core").astype(f32)
    step = (0, -1, 1, 2)[place]
    return along_z(both.astype(bf16), step).astype(f32) if step else both


def along(x, axis, step):
    return lax.ppermute(x, axis, [(i, (i + step) % 4) for i in range(4)])


def quad_exchange(x):
    me = lax.axis_index(QUAD)
    got = [lax.dynamic_index_in_dim(x, me, 0, keepdims=False)] + [
        lax.ppermute(
            lax.dynamic_index_in_dim(x, me ^ k, 0, keepdims=False),
            QUAD,
            [(i, i ^ k) for i in range(4)],
        )
        for k in (1, 2, 3)
    ]
    return jnp.stack([chosen(me ^ place, got) for place in range(4)])


def chosen(which, four):
    pair = [jnp.where(which % 2 == 0, four[k], four[k + 1]) for k in (0, 2)]
    return jnp.where(which < 2, pair[0], pair[1])


def ring_sum(x):
    me = lax.axis_index(ZRING)
    blocks = [lax.dynamic_index_in_dim(x, (me + k) % 4, 0, keepdims=False) for k in range(4)]
    back = [along_z(blocks[k], k).astype(f32) for k in (1, 2, 3)]
    return blocks[0].astype(f32) + (back[0] + back[1] + back[2])


def after(x, *others):
    return lax.optimization_barrier((x, *others))[0]


def gather_four(x, axis, dim):
    me = lax.axis_index(axis)
    out = jnp.zeros(x.shape[:dim] + (4,) + x.shape[dim:], x.dtype)
    for step in (1, -1, 2, 0):
        block = along(x, axis, step) if step else x
        out = lax.dynamic_update_index_in_dim(out, block, (me - step) % 4, dim)
    return out


def sum_four(x, axis):
    back = [along(x[k], axis, k) for k in (1, 2, 3)]
    return x[0].astype(f32) + (
        back[0].astype(f32) + back[1].astype(f32) + back[2].astype(f32)
    )


def plane_sum(x, first, second):
    x = x.reshape(4, 4, x.shape[0] // 16, x.shape[1])
    for axis in (first, second):
        dim = 1 if axis == "y" and axis == first else 0
        me = lax.axis_index(axis)
        blocks = [
            lax.dynamic_index_in_dim(x, (me + k) % 4, dim, keepdims=False) for k in range(4)
        ]
        x = sum_four([b.astype(bf16) for b in blocks], axis)
    return x.astype(bf16)


def mine_first(core, own, sib):
    return jnp.where(core == 0, own, sib), jnp.where(core == 0, sib, own)


def on_device(
    inputs,
    doc_ids,
    prenorm,
    query_proj,
    key_proj,
    value_proj,
    querynorm,
    keynorm,
    output_proj,
    postnorm,
    ffnnorm,
    gate_proj,
    up_proj,
    down_proj,
    endnorm,
    cotangent,
):
    core = lax.axis_index("core")
    tee = lax.axis_index("t")
    rows = prenorm.shape[0]
    head_rows = querynorm.shape[0]
    width = rows * 64
    tokens = inputs.shape[0]
    seq_length = doc_ids.shape[1]
    half_cols = HD // 2

    pos = lax.optimization_barrier(jnp.arange(width, dtype=jnp.int32))
    p_x, p_y, p_zh, p_in = (
        pos // (16 * rows),
        pos // (4 * rows) % 4,
        pos // (2 * rows) % 2,
        pos % (2 * rows),
    )
    natural = (p_x * 8 + p_zh * 4 + p_y) * (2 * rows) + p_in
    turn = (pos[:, None] == natural[None, :]).astype(bf16)

    kv_pair = (
        lax.dynamic_slice_in_dim(key_proj, tee * half_cols, half_cols, axis=1),
        lax.dynamic_slice_in_dim(value_proj, tee * half_cols, half_cols, axis=1),
    )
    out_t = output_proj.T
    gain_cols = jnp.stack(
        [
            prenorm,
            postnorm,
            ffnnorm,
            endnorm,
            jnp.pad(querynorm, (0, rows - head_rows)),
            jnp.pad(keynorm, (0, rows - head_rows)),
        ],
        axis=1,
    )
    gain_cols = jnp.pad(gain_cols, ((0, 0), (0, LANES - 6)))
    halves = [
        jnp.concatenate(
            [
                query_proj[:, c * HD : (c + 1) * HD],
                kv_pair[c],
                gain_cols,
                out_t[:, c * HD : (c + 1) * HD],
            ],
            axis=1,
        )
        for c in range(2)
    ]
    piece = halves[0].shape[1]
    keep, give = mine_first(core, halves[0], halves[1])
    got = swap(give, "core")
    first, second = mine_first(core, keep, got)
    attn_part = jnp.stack([first, second]).reshape(2 * rows, piece)
    both_z = jnp.stack(mine_first(lax.axis_index("zh"), attn_part, swap(attn_part, "zh")))
    attn_part = both_z.reshape(4 * rows, piece)
    attn_part, gate_proj, up_proj, down_proj = lax.optimization_barrier(
        (attn_part, gate_proj, up_proj, down_proj)
    )
    ff_cols = gate_proj.shape[1] // 4
    ff_pad = -(-ff_cols // LANES) * LANES

    def quarters(w):
        w = w.reshape(rows, 4, ff_cols).transpose(1, 0, 2)
        return jnp.pad(w, ((0, 0), (0, 0), (0, ff_pad - ff_cols)))

    ff_part = jnp.concatenate(
        [quarters(gate_proj), quarters(up_proj), quarters(down_proj.T)], axis=2
    )
    ff_part = quad_exchange(ff_part)
    o_at = piece - HD
    attn_part, ff_part = lax.optimization_barrier(
        (gather_four(attn_part, "y", 0), ff_part.reshape(4 * rows, 3 * ff_pad))
    )
    attn_half = gather_four(attn_part, "x", 0).reshape(width, piece)
    kv_to = HD + half_cols
    gain_all = attn_half[:, kv_to:o_at]

    own_w = attn_half[:, :kv_to]
    peer_w = swap(own_w, "t")
    qkv_w = (own_w, peer_w, swap(own_w, "core"), swap(peer_w, "core"))
    out_own = after(attn_half[:, o_at:], peer_w)
    out_peer = swap(out_own, "t")
    pick = (
        lax.broadcasted_iota(jnp.int32, (8, LANES), 0)
        == lax.broadcasted_iota(jnp.int32, (8, LANES), 1)
    ).astype(bf16)
    gain_rows = matmul_nt(pick, gain_all)
    pre_gain, post_gain, ffn_gain, end_gain = (gain_rows[k] for k in range(4))

    def head_gain(k):
        part = gain_rows[k].reshape(4, 4, 2, 2, rows)[..., :head_rows]
        return part.transpose(0, 2, 1, 3, 4).reshape(HD)

    qgain, kgain = head_gain(4), head_gain(5)

    ff_all = lax.all_gather(
        ff_part, PLANE, axis=0, tiled=True
    )
    gate_all, up_all, down_all = (
        ff_all[:, k * ff_pad : (k + 1) * ff_pad] for k in range(3)
    )

    resid = matmul(inputs, turn)
    grad_out = matmul(cotangent, turn)
    segment = doc_ids[0]
    order = jnp.arange(seq_length, dtype=jnp.int32)
    own_seg = lax.dynamic_slice_in_dim(segment, tee * tokens, tokens)
    own_at = tee * tokens + jnp.arange(tokens, dtype=jnp.int32)
    peer_seg = lax.dynamic_slice_in_dim(segment, (1 - tee) * tokens, tokens)
    peer_at = (1 - tee) * tokens + jnp.arange(tokens, dtype=jnp.int32)
    position = jnp.sum(
        jnp.where(
            (own_seg[:, None] == segment[None, :]) & (order[None, :] < own_at[:, None]), 1, 0
        ).astype(jnp.int32),
        axis=1,
    ).astype(f32)
    rates = jnp.exp(jnp.arange(HD // 2, dtype=f32) * (-2.0 * math.log(rope_base) / HD))
    angles = position[:, None] * rates[None, :]
    cos_tab, sin_tab = jnp.cos(angles), jnp.sin(angles)
    key_seg = jnp.concatenate([own_seg, peer_seg])
    key_at = jnp.concatenate([own_at, peer_at])
    allowed = (own_seg[:, None] == key_seg[None, :]) & (key_at[None, :] <= own_at[:, None])
    mask_rows = jnp.tile(allowed, (H, 1))

    normed_f, in_back = jax.vjp(rms_scale, resid, pre_gain)
    normed_in = normed_f.astype(bf16)
    n_qkv = 3 * HD
    qkv = [matmul(normed_in, w) for w in qkv_w]
    q_raw = jnp.stack([r[:, :HD] for r in qkv])
    kv = [
        jnp.concatenate(mine_first(tee, a[:, HD:], b[:, HD:]), axis=1)
        for a, b in (qkv[:2], qkv[2:])
    ]
    k_raw, v_raw = mine_first(core, kv[0], kv[1])
    q_full, q_back = jax.vjp(partial(head_piece, cos_tab, sin_tab, query_scale), q_raw, qgain)
    k_full, k_back = jax.vjp(partial(head_piece, cos_tab, sin_tab, 1.0), k_raw, kgain)
    query_rows = q_full.astype(bf16).reshape(H * tokens, HD)
    kv_own = jnp.concatenate([k_full.astype(bf16), v_raw.astype(bf16)], axis=1)
    kv_both = jnp.concatenate([kv_own, swap(kv_own, "t")], axis=0)
    out_peer = after(out_peer, kv_own)
    out_w = (out_own, out_peer, swap(out_own, "core"), swap(out_peer, "core"))
    keys_b, values_b = kv_both[:, :HD], kv_both[:, HD:]
    scores = matmul_nt(query_rows, keys_b)
    exp_scores = jnp.where(mask_rows, jnp.exp(scores), 0.0)
    log_total = jnp.log(jnp.sum(exp_scores, axis=1, keepdims=True))
    probs_f = jnp.where(mask_rows, jnp.exp(scores - log_total), 0.0)
    probs_b = probs_f.astype(bf16)
    mixed_rows = matmul(probs_b, values_b).astype(bf16)

    def head_of(x, h):
        return x[h * tokens : (h + 1) * tokens]

    def by_tee(four, dim):
        return jnp.concatenate(
            [*mine_first(tee, *four[:2]), *mine_first(tee, *four[2:])], axis=dim
        )

    branches = [matmul_nt(head_of(mixed_rows, h), out_w[h]) for h in range(H)]
    branch = (branches[0] + branches[1]) + (branches[2] + branches[3])
    mixed = by_tee([head_of(mixed_rows, h) for h in range(H)], 1)
    attn_norm, attn_back = jax.vjp(rms_scale, branch, post_gain)
    hidden = resid + attn_norm

    ff_norm, ff_in_back = jax.vjp(rms_scale, hidden, ffn_gain)

    def ff_forward(chunk):
        product, mix_back = jax.vjp(gelu_mix, matmul(chunk, gate_all), matmul(chunk, up_all))
        act = product.astype(bf16)
        return rows_first(matmul_nt(act, down_all)), act, mix_back

    ff_chunks = group_chunks(ff_norm.astype(bf16))
    done = [ff_forward(chunk) for chunk in ff_chunks]
    homes = [chunk_home(done[place][0], place) for place in range(4)]
    acts, mix_backs = [d[1] for d in done], [d[2] for d in done]
    ff_branch = homes[0] + (homes[1] + homes[2] + homes[3])
    end_norm, end_back = jax.vjp(rms_scale, ff_branch, end_gain)
    layer_out = matmul_nt((hidden + end_norm).astype(bf16), turn).astype(bf16)

    d_ff, grad_end = end_back(grad_out)

    def ff_backward(chunk, place):
        d_gate, d_up = mix_backs[place](matmul(chunk, down_all))
        d_gate, d_up = d_gate.astype(bf16), d_up.astype(bf16)
        d_chunk = matmul_nt(d_gate, gate_all) + matmul_nt(d_up, up_all)
        return rows_first(d_chunk), d_gate, d_up

    d_ff_chunks = group_chunks(d_ff.astype(bf16))
    done = [ff_backward(d_ff_chunks[place], place) for place in range(4)]
    homes = [chunk_home(done[place][0], place) for place in range(4)]
    ff_input, act, d_ff_rows, d_gate, d_up = (
        jnp.concatenate(lax.optimization_barrier(parts), axis=0)
        for parts in (
            ff_chunks,
            acts,
            d_ff_chunks,
            [d[1] for d in done],
            [d[2] for d in done],
        )
    )
    ff_input, act, d_ff_rows, d_gate, d_up, *_ = lax.optimization_barrier(
        (ff_input, act, d_ff_rows, d_gate, d_up, *(d[0] for d in done))
    )
    ff_grads = jnp.concatenate(
        [
            matmul_tn(ff_input, d_gate).astype(bf16),
            matmul_tn(ff_input, d_up).astype(bf16),
            matmul_tn(d_ff_rows, act).astype(bf16),
        ],
        axis=1,
    )
    d_ff_input = homes[0] + (homes[1] + homes[2] + homes[3])
    d_ff_input = after(d_ff_input, ff_grads, layer_out)
    ff_sums = lax.psum_scatter(rows_first(ff_grads), PLANE, scatter_dimension=0, tiled=True)
    d_h_part, grad_ffn = ff_in_back(d_ff_input)
    d_hidden = grad_out + d_h_part

    d_branch, grad_post = attn_back(d_hidden)
    d_branch_b = d_branch.astype(bf16)
    out_grad = rows_first(matmul_tn(d_branch_b, mixed).astype(bf16))
    d_mixed_rows = jnp.concatenate([matmul(d_branch_b, w).astype(bf16) for w in out_w], axis=0)
    delta = jnp.sum(
        d_mixed_rows.astype(f32) * mixed_rows.astype(f32), axis=1, keepdims=True
    )
    d_probs = matmul_nt(d_mixed_rows, values_b)
    d_scores = (probs_f * (d_probs - delta)).astype(bf16)
    d_queries = matmul(d_scores, keys_b).reshape(H, tokens, HD)
    d_kv = jnp.concatenate(
        [matmul_tn(d_scores, query_rows), matmul_tn(probs_b, d_mixed_rows)], axis=1
    )
    d_kv = d_kv[:tokens] + swap(d_kv[tokens:].astype(bf16), "t").astype(f32)
    d_keys, d_values = d_kv[:, :HD], d_kv[:, HD:]
    d_q_raw, grad_qgain = q_back(d_queries)
    d_k_raw, grad_kgain = k_back(d_keys)
    d_own, d_sib = mine_first(core, d_k_raw.astype(bf16), d_values.astype(bf16))
    d_q_b = d_q_raw.astype(bf16)
    d_side = [
        part
        for d in (d_own, d_sib)
        for part in mine_first(tee, d[:, :half_cols], d[:, half_cols:])
    ]
    d_q_two = by_tee([d_q_b[h] for h in range(H)], 1)
    d_qkv = jnp.concatenate(
        [d_q_two[:, : 2 * HD], d_own, d_q_two[:, 2 * HD :], d_sib], axis=1
    )
    qkv_grad = rows_first(matmul_tn(normed_in, d_qkv).astype(bf16))
    def core_sum(own, sib):
        return (own.astype(f32) + swap(sib, "core").astype(f32)).astype(bf16)

    qkv_cores = core_sum(qkv_grad[:, :n_qkv], qkv_grad[:, n_qkv:])
    qkv_cores, *late = lax.optimization_barrier((qkv_cores, *d_side, *(d_q_b[h] for h in range(H))))
    d_normeds = [
        matmul_nt(jnp.concatenate([late[H + h], late[h]], axis=1), qkv_w[h]) for h in range(H)
    ]
    d_normed = (d_normeds[0] + d_normeds[1]) + (d_normeds[2] + d_normeds[3])
    d_in_part, grad_pre = in_back(d_normed)
    inputs_grad = jnp.dot(
        d_hidden + d_in_part,
        turn.T.astype(f32),
        precision=lax.Precision.HIGHEST,
        preferred_element_type=f32,
    )

    def turned_head(grad):
        grad = grad.reshape(4, 2, 4, 2, head_rows).transpose(0, 2, 1, 3, 4)
        return jnp.pad(grad, ((0, 0),) * 4 + ((0, rows - head_rows),)).reshape(width)

    gain_sets = [
        jnp.pad(jnp.stack(three), ((0, 5), (0, 0))).astype(bf16)
        for three in (
            (grad_pre, grad_post, grad_ffn),
            (grad_end, turned_head(grad_qgain), turned_head(grad_kgain)),
        )
    ]
    gain_own, gain_sib = (
        matmul_tn(g, pick).astype(bf16) for g in mine_first(core, gain_sets[0], gain_sets[1])
    )

    qkv_sum = plane_sum(qkv_cores, "y", "x")
    out_sum = plane_sum(
        core_sum(
            jnp.concatenate([out_grad[:, : 2 * HD], gain_own], axis=1),
            jnp.concatenate([out_grad[:, 2 * HD :], gain_sib], axis=1),
        ),
        "x",
        "y",
    )
    qkv_sum, out_sum, ff_sums, inputs_grad = lax.optimization_barrier(
        (qkv_sum, out_sum, ff_sums, inputs_grad)
    )
    ff_sums = quad_exchange(ff_sums.reshape(4, rows, 3 * ff_pad))

    def joined(k):
        part = ff_sums[:, :, k * ff_pad : k * ff_pad + ff_cols]
        return part.transpose(1, 0, 2).reshape(rows, 4 * ff_cols).astype(f32)

    sent_gate, sent_up, sent_down = joined(0), joined(1), joined(2).T
    shared = (qkv_sum[:, 2 * HD :], out_sum[:, 2 * HD :])
    for_tee = [
        jnp.concatenate(
            [part[:, k * HD : (k + 1) * HD] for part in (qkv_sum, out_sum)] + [*shared],
            axis=1,
        ).reshape(2, 1, 2 * rows, 3 * HD + LANES)
        for k in range(2)
    ]
    sums = jnp.concatenate(for_tee, axis=1).reshape(4, 2 * rows, 3 * HD + LANES)
    sums = ring_sum(sums).reshape(2, rows, 3 * HD + LANES)
    own, theirs = mine_first(core, sums[0], sums[1])
    sum_0, sum_1 = mine_first(core, own, swap(theirs, "core"))
    sent_query = jnp.concatenate([sum_0[:, :HD], sum_1[:, :HD]], axis=1)
    sent_outw = jnp.concatenate([sum_0[:, HD : 2 * HD], sum_1[:, HD : 2 * HD]], axis=1).T
    sent_key, sent_value = sum_0[:, 2 * HD : 3 * HD], sum_1[:, 2 * HD : 3 * HD]
    sent_pre, sent_post, sent_ffn = (sum_0[:, 3 * HD + k] for k in range(3))
    sent_end = sum_1[:, 3 * HD]
    sent_qgain, sent_kgain = (sum_1[:head_rows, 3 * HD + k] for k in (1, 2))
    return (
        layer_out,
        inputs_grad,
        sent_pre,
        sent_query,
        sent_key,
        sent_value,
        sent_qgain,
        sent_kgain,
        sent_outw,
        sent_post,
        sent_ffn,
        sent_gate,
        sent_up,
        sent_down,
        sent_end,
    )


def solution(mesh):
    parts = Mesh(mesh.devices.reshape(SIZES), AXES)
    every = (*DP, "t")
    return jax.shard_map(
        on_device,
        mesh=parts,
        in_specs=(
            P(every, None),
            P(DP, None),
            P(DP),
            P(DP, "t"),
            P(DP, None),
            P(DP, None),
            P(DP),
            P(DP),
            P("t", DP),
            P(DP),
            P(DP),
            P(DP, "t"),
            P(DP, "t"),
            P("t", DP),
            P(DP),
            P(every, None),
        ),
        out_specs=(
            P(every, None),
            P(every, None),
            P(DP),
            P(DP, "t"),
            P(DP, None),
            P(DP, None),
            P(DP),
            P(DP),
            P("t", DP),
            P(DP),
            P(DP),
            P(DP, "t"),
            P(DP, "t"),
            P("t", DP),
            P(DP),
        ),
        check_vma=False,
    )
```
